32 devices in a mesh: dp: 8 (over y, x, core), tensor: 4 (over z).
Axes of the slice: x: 2, y: 2, z: 4, core: 2. Of those that a mesh axis runs over, the one named last changes fastest.
Arguments:
- tokens: bfloat16 [16384, 1024], P(('dp', 'tensor')), may hold values from -6 to 6
- lengths: int32 [16], P('dp'), may hold values from 256 to 1024, as said below
- starts: int32 [16], P('dp'), may hold values from 0 to 768, as said below
- norm_one: float32 [1024], replicated, may hold values from 0.1 to 1.9
- w_query: bfloat16 [1024, 1024], P('dp', 'tensor'), may hold values from -0.1875 to 0.1875
- w_key: bfloat16 [1024, 1024], P('dp', 'tensor'), may hold values from -0.1875 to 0.1875
- w_value: bfloat16 [1024, 2048], P('dp', 'tensor'), may hold values from -0.1875 to 0.1875
- w_gating: bfloat16 [1024, 2048], P('dp', 'tensor'), may hold values from -0.1875 to 0.1875
- w_decay: bfloat16 [1024, 8], P('dp', 'tensor'), may hold values from -0.1875 to 0.1875
- w_strength: bfloat16 [1024, 8], P('dp', 'tensor'), may hold values from -0.1875 to 0.1875
- filter_query: float32 [4, 1024], replicated, may hold values from -3 to 3
- filter_key: float32 [4, 1024], replicated, may hold values from -3 to 3
- filter_value: float32 [4, 2048], replicated, may hold values from -3 to 3
- decay_log: float32 [8], replicated, may hold values from -1 to 2.5
- decay_bias: float32 [8], replicated, may hold values from -6 to -1
- head_gain: float32 [256], replicated, may hold values from 0.1 to 1.9
- w_output: bfloat16 [2048, 1024], P('tensor', 'dp'), may hold values from -0.25 to 0.25
- norm_two: float32 [1024], replicated, may hold values from 0.1 to 1.9
- w_gate: bfloat16 [1024, 2816], P('dp', 'tensor'), may hold values from -0.1875 to 0.1875
- w_up: bfloat16 [1024, 2816], P('dp', 'tensor'), may hold values from -0.1875 to 0.1875
- w_down: bfloat16 [2816, 1024], P('tensor', 'dp'), may hold values from -0.15625 to 0.15625
- cotangent: bfloat16 [16384, 1024], P(('dp', 'tensor')), may hold values from -6 to 6
Outputs:
- block_out: bfloat16 [16384, 1024], P(('dp', 'tensor'))
- grad_tokens: float32 [16384, 1024], P(('dp', 'tensor'))
- grad_norm_one: float32 [1024], replicated
- grad_w_query: float32 [1024, 1024], P('dp', 'tensor')
- grad_w_key: float32 [1024, 1024], P('dp', 'tensor')
- grad_w_value: float32 [1024, 2048], P('dp', 'tensor')
- grad_w_gating: float32 [1024, 2048], P('dp', 'tensor')
- grad_w_decay: float32 [1024, 8], P('dp', 'tensor')
- grad_w_strength: float32 [1024, 8], P('dp', 'tensor')
- grad_filter_query: float32 [4, 1024], replicated
- grad_filter_key: float32 [4, 1024], replicated
- grad_filter_value: float32 [4, 2048], replicated
- grad_decay_log: float32 [8], replicated
- grad_decay_bias: float32 [8], replicated
- grad_head_gain: float32 [256], replicated
- grad_w_output: float32 [2048, 1024], P('tensor', 'dp')
- grad_norm_two: float32 [1024], replicated
- grad_w_gate: float32 [1024, 2816], P('dp', 'tensor')
- grad_w_up: float32 [1024, 2816], P('dp', 'tensor')
- grad_w_down: float32 [2816, 1024], P('tensor', 'dp')
The draws below stay inside these ranges and needn't reach their ends.
Inputs may be any that keep to these rules, and one draw needn't show every extreme that they name: lengths[0] = 1024 and lengths[1] = 256. starts[r] + lengths[r] <= 1024; starts[1] = 768.
All inputs are finite; a program needn't handle non-finite values.
Results may differ from the reference program's by a relative error of at most 0.013.
Values may be sent and summed in bfloat16 or wider, within the bound.
No kernel may reach another device: no remote copies, remote signals or barrier semaphores. Data moves between devices by JAX's collectives and lax.ppermute only.
A program may use at most 256 MiB of HBM per device.

```python
import jax
import jax.numpy as jnp
from jax import lax

D = 1024
H = 8
DK = 128
DV = 256
FF = 2816
CONV = 4
SPAN = 64
SLOT = 1024
MINLEN = 256
ROWS = 16
TOKENS = 16384


def ragged_pair(key):
    key_length = jax.random.fold_in(key, 11)
    key_start = jax.random.fold_in(key, 12)
    lengths = jax.random.randint(key_length, (ROWS,), MINLEN, SLOT + 1)
    lengths = lengths.at[0].set(SLOT).at[1].set(MINLEN)
    room = SLOT - lengths + 1
    starts = jax.random.randint(key_start, (ROWS,), 0, room)
    starts = starts.at[1].set(SLOT - MINLEN)
    return (lengths.astype(jnp.int32), starts.astype(jnp.int32))


def draw_lengths(key, part):
    return ragged_pair(key)[0]


def draw_starts(key, part):
    return ragged_pair(key)[1]


def block_levels(rng, shape, split, smallest, largest):
    def one(position, parts):
        steps = jax.random.uniform(jax.random.fold_in(jax.random.fold_in(rng, 6), position), (parts,), jnp.float32, smallest / len(split), largest / len(split))
        return jnp.repeat(jnp.exp(steps), shape[position] // parts).reshape((-1,) + (1,) * (len(shape) - position - 1))

    factor_of = one(*split[0])
    for cut in split[1:]:
        factor_of = factor_of * one(*cut)
    return factor_of


def bell_draw(stream_key, extent, scale, limit, cuts=(), kind=jnp.bfloat16):
    level = block_levels(stream_key, extent, cuts, -0.22, 0.18) if cuts else 1.0
    values = jax.random.normal(stream_key, extent, jnp.float32) * scale * level
    return jnp.minimum(jnp.maximum(values, -limit), limit).astype(kind)


def setup_inputs(seed: int = 0) -> dict:
    key_list = jax.random.split(jax.random.key(seed), 23)
    return {
        "tokens": bell_draw(key_list[0], (TOKENS, D), 1.0, 6.0, ((0, 32),)),
        "lengths": draw_lengths(jax.random.fold_in(key_list[22], 71), 0),
        "starts": draw_starts(jax.random.fold_in(key_list[22], 71), 0),
        "norm_one": jnp.clip(1.0 + 0.18 * jax.random.normal(key_list[3], (D,), jnp.float32), 0.1, 1.9),
        "w_query": bell_draw(key_list[4], (D, H * DK), D ** -0.5, 0.1875, ((0, 8), (1, 4))),
        "w_key": bell_draw(key_list[5], (D, H * DK), D ** -0.5, 0.1875, ((0, 8), (1, 4))),
        "w_value": bell_draw(key_list[6], (D, H * DV), D ** -0.5, 0.1875, ((0, 8), (1, 4))),
        "w_gating": bell_draw(key_list[7], (D, H * DV), D ** -0.5, 0.1875, ((0, 8), (1, 4))),
        "w_decay": bell_draw(key_list[8], (D, H), D ** -0.5, 0.1875, ((0, 8), (1, 4))),
        "w_strength": bell_draw(key_list[9], (D, H), D ** -0.5, 0.1875, ((0, 8), (1, 4))),
        "filter_query": bell_draw(key_list[10], (CONV, H * DK), 0.5, 3.0, (), jnp.float32),
        "filter_key": bell_draw(key_list[11], (CONV, H * DK), 0.5, 3.0, (), jnp.float32),
        "filter_value": bell_draw(key_list[12], (CONV, H * DV), 0.5, 3.0, (), jnp.float32),
        "decay_log": jnp.clip(jax.random.uniform(key_list[13], (H,), jnp.float32, -1.0, 2.5), -1.0, 2.5),
        "decay_bias": jnp.clip(jax.random.uniform(key_list[14], (H,), jnp.float32, -6.0, -1.0), -6.0, -1.0),
        "head_gain": jnp.clip(1.0 + 0.18 * jax.random.normal(key_list[15], (DV,), jnp.float32), 0.1, 1.9),
        "w_output": bell_draw(key_list[16], (H * DV, D), (H * DV // 4) ** -0.5, 0.25, ((0, 4), (1, 8))),
        "norm_two": jnp.clip(1.0 + 0.18 * jax.random.normal(key_list[17], (D,), jnp.float32), 0.1, 1.9),
        "w_gate": bell_draw(key_list[18], (D, FF), D ** -0.5, 0.1875, ((0, 8), (1, 4))),
        "w_up": bell_draw(key_list[19], (D, FF), D ** -0.5, 0.1875, ((0, 8), (1, 4))),
        "w_down": bell_draw(key_list[20], (FF, D), (FF // 2) ** -0.5, 0.15625, ((0, 4), (1, 8))),
        "cotangent": bell_draw(key_list[21], (TOKENS, D), 1.0, 6.0, ((0, 32),)),
    }


@jax.custom_vjp
def low(v):
    return lax.optimization_barrier(v.astype(jnp.bfloat16)).astype(jnp.float32)

@jax.custom_vjp
def low_back(v):
    return v

def low_keep(v):
    return (low(v), None)

def low_pass(kept, grad):
    return (grad,)

def back_keep(v):
    return (v, None)

def back_low(kept, grad):
    return (low(grad),)
low.defvjp(low_keep, low_pass)
low_back.defvjp(back_keep, back_low)

def matmul(left, right):
    return jnp.dot(left, right, precision=lax.Precision.HIGHEST)

def rmsnorm(values, gain):
    return values * lax.rsqrt(lax.optimization_barrier(jnp.mean(values * values, -1, keepdims=True)) + 1e-05) * gain

def causal_filter(inputs, taps):
    length = inputs.shape[1]
    width = taps.shape[0]
    padded = jnp.pad(inputs, ((0, 0), (width - 1, 0), (0, 0)))
    total = jnp.zeros_like(inputs)
    for offset in range(width):
        total = total + taps[offset] * padded[:, offset:offset + length]
    return jax.nn.silu(total)

def unit_rows(values):
    return values * lax.rsqrt(lax.optimization_barrier(jnp.sum(values * values, -1, keepdims=True)) + 1e-06)

def span_rule(queries, keys, values, writes, decays):
    rows, heads, length, kdim = queries.shape
    vdim = values.shape[-1]
    count = length // SPAN
    highest = lax.Precision.HIGHEST

    def blocks(array):
        shaped = array.reshape((rows, heads, count, SPAN) + array.shape[3:])
        return jnp.moveaxis(shaped, 2, 0)
    strict = jnp.tril(jnp.ones((SPAN, SPAN), jnp.float32), -1)
    causal = jnp.tril(jnp.ones((SPAN, SPAN), jnp.float32))
    identity = jnp.eye(SPAN, dtype=jnp.float32)

    def advance(state, block):
        block_q, block_k, block_v, block_w, block_d = block
        cumulative = jnp.cumsum(block_d, -1)
        spread = jnp.exp(jnp.minimum(cumulative[..., :, None] - cumulative[..., None, :], 0.0))
        keys_keys = jnp.einsum('rhid,rhjd->rhij', block_k, block_k, precision=highest)
        system = identity + block_w[..., :, None] * spread * keys_keys * strict
        growth = jnp.exp(cumulative)
        source = block_w[..., None] * block_v - (block_w * growth)[..., None] * jnp.einsum('rhid,rhde->rhie', block_k, state, precision=highest)
        delta = lax.linalg.triangular_solve(system, source, left_side=True, lower=True)
        scores = jnp.einsum('rhid,rhjd->rhij', block_q, block_k, precision=highest) * spread * causal
        emitted = growth[..., None] * jnp.einsum('rhid,rhde->rhie', block_q, state, precision=highest)
        emitted = emitted + jnp.einsum('rhij,rhje->rhie', scores, delta, precision=highest)
        remain = jnp.exp(cumulative[..., -1:] - cumulative)
        new_state = jnp.exp(cumulative[..., -1])[..., None, None] * state
        new_state = new_state + jnp.einsum('rhid,rhie->rhde', block_k * remain[..., None], delta, precision=highest)
        return (new_state, emitted)
    start_state = jnp.zeros((rows, heads, kdim, vdim), jnp.float32)
    _, outputs = lax.scan(jax.checkpoint(advance), start_state, (blocks(queries), blocks(keys), blocks(values), blocks(writes), blocks(decays)))
    return jnp.moveaxis(outputs, 0, 2).reshape(rows, heads, length, vdim)

def mixing(proj_query, proj_key, proj_value, proj_gate, proj_decay, proj_strength, filter_query, filter_key, filter_value, decay_log, decay_bias, head_gain, row_mask):
    rows, length = row_mask.shape
    heads = proj_decay.shape[-1]
    valid = row_mask[..., None]
    queries = causal_filter(proj_query * valid, filter_query).reshape(rows, length, heads, DK)
    keys = causal_filter(proj_key * valid, filter_key).reshape(rows, length, heads, DK)
    values = causal_filter(proj_value * valid, filter_value).reshape(rows, length, heads, DV)
    queries = unit_rows(queries) * DK ** (-0.5)
    keys = unit_rows(keys) * valid[..., None]
    writes = jax.nn.sigmoid(proj_strength) * valid
    decays = -jnp.exp(decay_log) * jax.nn.softplus(proj_decay + decay_bias) * valid
    outputs = span_rule(jnp.moveaxis(queries, 2, 1), jnp.moveaxis(keys, 2, 1), jnp.moveaxis(values, 2, 1), jnp.moveaxis(writes, 2, 1), jnp.moveaxis(decays, 2, 1))
    outputs = jnp.moveaxis(outputs, 1, 2)
    outputs = outputs * lax.rsqrt(lax.optimization_barrier(jnp.mean(outputs * outputs, -1, keepdims=True)) + 1e-05) * head_gain
    gating = jax.nn.silu(proj_gate).reshape(rows, length, heads, DV)
    return (outputs * gating * valid[..., None]).reshape(rows, length, heads * DV)

def forward(inputs, row_mask, norm_one, w_query, w_key, w_value, w_gating, w_decay, w_strength, filter_query, filter_key, filter_value, decay_log, decay_bias, head_gain, w_output, norm_two, w_gate, w_up, w_down):
    normed_one = low(rmsnorm(inputs, norm_one))
    proj_query = low_back(matmul(normed_one, w_query))
    proj_key = low_back(matmul(normed_one, w_key))
    proj_value = low_back(matmul(normed_one, w_value))
    proj_gate = low_back(matmul(normed_one, w_gating))
    proj_decay = low_back(matmul(normed_one, w_decay))
    proj_strength = low_back(matmul(normed_one, w_strength))
    mixed = mixing(proj_query, proj_key, proj_value, proj_gate, proj_decay, proj_strength, filter_query, filter_key, filter_value, decay_log, decay_bias, head_gain, row_mask)
    attention = low_back(matmul(low(mixed), w_output))
    middle = inputs + attention
    normed_two = low(rmsnorm(middle, norm_two))
    gate = low_back(matmul(normed_two, w_gate))
    upward = low_back(matmul(normed_two, w_up))
    hidden = low(jax.nn.silu(gate) * upward)
    feed = low_back(matmul(hidden, w_down))
    return row_mask[..., None] * (middle + feed)

def reference(tokens, lengths, starts, norm_one, w_query, w_key, w_value, w_gating, w_decay, w_strength, filter_query, filter_key, filter_value, decay_log, decay_bias, head_gain, w_output, norm_two, w_gate, w_up, w_down, cotangent):
    params = tuple((p.astype(jnp.float32) for p in (norm_one, w_query, w_key, w_value, w_gating, w_decay, w_strength, filter_query, filter_key, filter_value, decay_log, decay_bias, head_gain, w_output, norm_two, w_gate, w_up, w_down)))
    group = 4 if ROWS % 4 == 0 else 2 if ROWS % 2 == 0 else 1
    slot_pos = jnp.arange(SLOT, dtype=jnp.int32)
    row_mask = ((slot_pos[None, :] >= starts[:, None]) & (slot_pos[None, :] < (starts + lengths)[:, None])).astype(jnp.float32)
    inputs = tokens.astype(jnp.float32).reshape(ROWS // group, group, SLOT, D)
    upstream = cotangent.astype(jnp.float32).reshape(ROWS // group, group, SLOT, D)
    masks = row_mask.reshape(ROWS // group, group, SLOT)

    def group_step(totals, batch):
        group_in, group_cot, group_mask = batch

        def forward_group(values, *weights):
            return forward(values, group_mask, *weights)
        output, pull = jax.vjp(forward_group, group_in, *params)
        pulled = pull(group_cot)
        return (tuple((t + g for t, g in zip(totals, pulled[1:]))), (output, pulled[0]))
    totals, (outputs, input_grads) = lax.scan(group_step, tuple((jnp.zeros_like(p) for p in params)), (inputs, upstream, masks))
    g_norm_one, g_query, g_key, g_value, g_gating, g_decay, g_strength, g_filter_query, g_filter_key, g_filter_value, g_decay_log, g_decay_bias, g_head_gain, g_output, g_norm_two, g_gate, g_up, g_down = totals
    return (outputs.reshape(TOKENS, D).astype(jnp.bfloat16), input_grads.reshape(TOKENS, D), g_norm_one, g_query, g_key, g_value, g_gating, g_decay, g_strength, g_filter_query, g_filter_key, g_filter_value, g_decay_log, g_decay_bias, g_head_gain, g_output, g_norm_two, g_gate, g_up, g_down)
```

```python
import functools
import jax
import jax.numpy as jnp
from jax import lax
from jax.experimental import pallas as pl
from jax.experimental.pallas import tpu as pltpu
from jax.sharding import PartitionSpec as P

DK = 128
DV = 256
SLOT = 1024
LANES = 128
BLOCK = 256
F32 = jnp.float32
BF16 = jnp.bfloat16


def dot(left, right, dim_left, dim_right):
    return lax.dot_general(
        left, right, (((dim_left,), (dim_right,)), ((), ())), preferred_element_type=F32
    )


def halves(value):
    high = value.astype(BF16)
    return high, (value - high.astype(F32)).astype(BF16)


def mm(left, right, dim_left=1, dim_right=0):
    left_high, left_low = halves(left)
    right_high, right_low = halves(right)
    return (
        dot(left_high, right_high, dim_left, dim_right)
        + dot(left_high, right_low, dim_left, dim_right)
        + dot(left_low, right_high, dim_left, dim_right)
    )


def mm_full(left, right, dim_left, dim_right):
    return lax.dot_general(
        left,
        right,
        (((dim_left,), (dim_right,)), ((), ())),
        preferred_element_type=F32,
        precision=lax.Precision.HIGHEST,
    )


def sigmoid(value):
    return 1.0 / (1.0 + jnp.exp(-value))


def softplus(value):
    return jnp.maximum(value, 0.0) + jnp.log1p(jnp.exp(-jnp.abs(value)))


def valid_rows(first, count, start, end):
    position = first + lax.broadcasted_iota(jnp.int32, (count, 1), 0)
    return jnp.where((position >= start) & (position < end), 1.0, 0.0).astype(F32)


def convolve(extended, taps, count):
    total = taps[0:1, :] * extended[5 : 5 + count]
    for offset in range(1, 4):
        total = total + taps[offset : offset + 1, :] * extended[5 + offset : 5 + offset + count]
    return total


def unit_scale(value):
    return lax.rsqrt(jnp.sum(value * value, -1, keepdims=True) + 1e-06)


def triangle(size):
    row = lax.broadcasted_iota(jnp.int32, (size, size), 0)
    column = lax.broadcasted_iota(jnp.int32, (size, size), 1)
    return row, column


def lower_ones(size):
    row, column = triangle(size)
    return jnp.where(row >= column, 1.0, 0.0).astype(F32)


def inverses(systems, size):
    row, column = triangle(size)
    differ = jnp.bitwise_xor(row, column)
    eye = jnp.where(differ == 0, 1.0, 0.0).astype(F32)
    found = [eye - jnp.where(differ == 1, system, 0.0) for system in systems]
    width = 2
    while width < size:
        mask = (differ >= width) & (differ < 2 * width)
        parts = [jnp.where(mask, system, 0.0) for system in systems]
        middle = [mm(f, p) for f, p in zip(found, parts)]
        found = [f - mm(m, f) for f, m in zip(found, middle)]
        width *= 2
    return found


def gather_inputs(first, start, end, refs, heads, block):
    pre_q, pre_k, pre_v, pre_ab, halo_q, halo_k, halo_v, taps_q, taps_k, taps_v, rate, bias = refs
    valid = valid_rows(first, block, start, end)
    halo_valid = valid_rows(first - 8, 8, start, end)
    ext_q = jnp.concatenate([halo_q[...] * halo_valid, pre_q[...] * valid], 0)
    ext_k = jnp.concatenate([halo_k[...] * halo_valid, pre_k[...] * valid], 0)
    ext_v = jnp.concatenate([halo_v[...] * halo_valid, pre_v[...] * valid], 0)
    conv_q = convolve(ext_q, taps_q[...], block)
    conv_k = convolve(ext_k, taps_k[...], block)
    conv_v = convolve(ext_v, taps_v[...], block)
    both = pre_ab[...]
    shifted = both + bias[...]
    decay = rate[...] * softplus(shifted) * valid
    strength = sigmoid(both) * valid
    ones = lower_ones(block)
    cum = mm_full(ones, decay, 1, 0)
    cum_rows = mm_full(decay, ones, 0, 1)
    return dict(
        valid=valid, ext=(ext_q, ext_k, ext_v), conv=(conv_q, conv_k, conv_v), shifted=shifted,
        decay=decay, strength=strength, ones=ones, cum=cum, cum_rows=cum_rows,
    )


def head_operands(common, head, heads, block):
    conv_q, conv_k, conv_v = common["conv"]
    keys = slice(head * DK, (head + 1) * DK)
    vals = slice(head * DV, (head + 1) * DV)
    u_q, u_k, u_v = conv_q[:, keys], conv_k[:, keys], conv_v[:, vals]
    s_q, s_k, s_v = sigmoid(u_q), sigmoid(u_k), sigmoid(u_v)
    y_q, y_k = u_q * s_q, u_k * s_k
    n_q, n_k = unit_scale(y_q), unit_scale(y_k)
    cum = common["cum"][:, head : head + 1]
    cum_row = common["cum_rows"][head : head + 1, :]
    last = common["cum"][block - 1 : block, head : head + 1]
    spread = jnp.exp(jnp.minimum(cum - cum_row, 0.0))
    return dict(
        u=(u_q, u_k, u_v), s=(s_q, s_k, s_v), n=(n_q, n_k), unit=(y_q * n_q, y_k * n_k),
        q=y_q * (n_q * DK ** (-0.5)), k=y_k * (n_k * common["valid"]), v=u_v * s_v,
        beta=common["strength"][:, heads + head : heads + head + 1],
        growth=jnp.exp(cum), remain=jnp.exp(last - cum), whole=jnp.exp(last), spread=spread,
    )


def forward_kernel(heads, block, bounds, pre_q, pre_k, pre_v, pre_g, pre_ab, halo_q, halo_k, halo_v,
                   taps_q, taps_k, taps_v, rate, bias, gain, mixed, out, states, deltas, solves, state):
    row, step = pl.program_id(0), pl.program_id(1)

    @pl.when(step == 0)
    def _():
        state[...] = jnp.zeros_like(state)

    refs = (pre_q, pre_k, pre_v, pre_ab, halo_q, halo_k, halo_v, taps_q, taps_k, taps_v, rate, bias)
    common = gather_inputs(step * block, bounds[0, row], bounds[1, row], refs, heads, block)
    ops = [head_operands(common, head, heads, block) for head in range(heads)]
    at, to = triangle(block)
    systems = [jnp.where(at > to, o["beta"] * o["spread"] * mm(o["k"], o["k"], 1, 1), 0.0) for o in ops]
    found = inverses(systems, block)
    for head, o in enumerate(ops):
        vals = slice(head * DV, (head + 1) * DV)
        old = state[head]
        states[head] = old.astype(states.dtype)
        source = o["beta"] * o["v"] - (o["beta"] * o["growth"]) * mm(o["k"], old)
        delta = mm(found[head], source)
        scores = jnp.where(at >= to, o["spread"] * mm(o["q"], o["k"], 1, 1), 0.0)
        emitted = o["growth"] * mm(o["q"], old) + mm(scores, delta)
        state[head] = o["whole"] * old + mm(o["k"] * o["remain"], delta, 0, 0)
        solves[head] = found[head].astype(solves.dtype)
        deltas[:, vals] = delta.astype(deltas.dtype)
        out[:, vals] = emitted.astype(out.dtype)
        scale = lax.rsqrt(jnp.mean(emitted * emitted, -1, keepdims=True) + 1e-05)
        gate = pre_g[:, vals]
        mixed[:, vals] = (
            emitted * scale * gain[...] * (gate * sigmoid(gate)) * common["valid"]
        ).astype(mixed.dtype)


def backward_kernel(heads, block, steps, bounds, pre_q, pre_k, pre_v, pre_g, pre_ab, halo_q, halo_k, halo_v,
                    taps_q, taps_k, taps_v, rate, bias, gain, out, states, deltas, solves, grad,
                    d_q, d_k, d_v, d_g, d_ab, d_taps_q, d_taps_k, d_taps_v, d_small, d_gain,
                    d_state, next_q, next_k, next_v):
    row, back = pl.program_id(0), pl.program_id(1)
    step = steps - 1 - back

    @pl.when((row == 0) & (back == 0))
    def _():
        for ref in (d_taps_q, d_taps_k, d_taps_v, d_small, d_gain):
            ref[...] = jnp.zeros_like(ref)

    @pl.when(back == 0)
    def _():
        for ref in (d_state, next_q, next_k, next_v):
            ref[...] = jnp.zeros_like(ref)

    refs = (pre_q, pre_k, pre_v, pre_ab, halo_q, halo_k, halo_v, taps_q, taps_k, taps_v, rate, bias)
    common = gather_inputs(step * block, bounds[0, row], bounds[1, row], refs, heads, block)
    valid = common["valid"]
    at, to = triangle(block)
    lane = lax.broadcasted_iota(jnp.int32, (block, LANES), 1)
    ones_cols = jnp.ones((block, LANES), BF16)
    d_cum = jnp.zeros((block, LANES), F32)
    d_last = jnp.zeros((1, LANES), F32)
    d_beta = jnp.zeros((block, LANES), F32)
    du_q, du_k, du_v = [], [], []
    gain_sum = jnp.zeros((1, DV), F32)
    for head in range(heads):
        o = head_operands(common, head, heads, block)
        vals = slice(head * DV, (head + 1) * DV)
        q, k, v, beta, growth, remain, whole, spread = (
            o[name] for name in ("q", "k", "v", "beta", "growth", "remain", "whole", "spread"))
        emitted = out[:, vals].astype(F32)
        scale = lax.rsqrt(jnp.mean(emitted * emitted, -1, keepdims=True) + 1e-05)
        unit = emitted * scale
        gate = pre_g[:, vals]
        s_g = sigmoid(gate)
        d_mixed = grad[:, vals].astype(F32) * valid
        d_g[:, vals] = (d_mixed * unit * gain[...] * (s_g * (1.0 + gate * (1.0 - s_g)))).astype(d_g.dtype)
        part = d_mixed * (gate * s_g)
        gain_sum = gain_sum + jnp.sum(part * unit, 0, keepdims=True)
        weighted = part * gain[...]
        d_out = scale * (weighted - unit * jnp.mean(weighted * unit, -1, keepdims=True))
        old = states[head].astype(F32)
        delta = deltas[:, vals]
        solve = solves[head]
        d_new = d_state[head]
        q_k = mm(q, k, 1, 1)
        k_k = mm(k, k, 1, 1)
        scores = jnp.where(at >= to, spread * q_k, 0.0)
        linked = jnp.where(at > to, spread * k_k, 0.0)
        k_s = mm(k, old)
        q_s = mm(q, old)
        k_rem = k * remain
        d_delta = mm(scores, d_out, 0, 0) + mm(k_rem, d_new)
        d_source = mm(solve, d_delta, 0, 0)
        d_system = -mm(d_source, delta, 1, 1)
        d_scores = mm(d_out, delta, 1, 1)
        d_qk = jnp.where(at >= to, d_scores * spread, 0.0)
        by_link = d_system * linked
        d_kk = jnp.where(at > to, beta * d_system * spread, 0.0)
        edge, edge_low = halves(d_scores * scores + beta * by_link)
        d_query = growth * mm(d_out, old, 1, 1) + mm(d_qk, k)
        back_state = mm(delta, d_new, 1, 1)
        d_key = (
            mm((beta * growth) * d_source, old, 1, 1) * (-1.0)
            + mm(d_qk, q, 0, 0)
            + mm(d_kk, k)
            + mm(d_kk, k, 0, 0)
            + remain * back_state
        )
        d_value = beta * d_source
        lose = jnp.sum(k_rem * back_state, -1, keepdims=True)
        pull = jnp.sum(d_source * k_s, -1, keepdims=True)
        grow = growth * (jnp.sum(d_out * q_s, -1, keepdims=True) - beta * pull)
        d_b = jnp.sum(d_source * v, -1, keepdims=True) - growth * pull + jnp.sum(by_link, -1, keepdims=True)
        cut = (
            dot(edge, ones_cols, 1, 0) - dot(edge, ones_cols, 0, 0)
            + dot(edge_low, ones_cols, 1, 0) - dot(edge_low, ones_cols, 0, 0)
        )
        d_cum = jnp.where(lane == head, cut + (grow - lose), d_cum)
        d_beta = jnp.where(lane == heads + head, d_b, d_beta)
        total = jnp.sum(lose, keepdims=True) + whole * jnp.sum(old * d_new, keepdims=True)
        d_last = jnp.where(lane[0:1] == head, total, d_last)
        d_state[head] = (
            whole * d_new + mm(q, growth * d_out, 0, 0) - mm(k * (beta * growth), d_source, 0, 0)
        )
        unit_q, unit_k = o["unit"]
        n_q, n_k = o["n"]
        d_unit = d_query * DK ** (-0.5)
        d_yq = n_q * (d_unit - unit_q * jnp.sum(unit_q * d_unit, -1, keepdims=True))
        d_unit = d_key * valid
        d_yk = n_k * (d_unit - unit_k * jnp.sum(unit_k * d_unit, -1, keepdims=True))
        for store, d_y, u, s in zip((du_q, du_k, du_v), (d_yq, d_yk, d_value), o["u"], o["s"]):
            store.append(d_y * (s * (1.0 + u * (1.0 - s))))
    d_decay = mm_full(common["ones"], d_cum, 0, 0) + d_last
    slope = d_decay * rate[...] * sigmoid(common["shifted"]) * valid
    strength = common["strength"]
    d_pre_b = d_beta * strength * (1.0 - strength)
    d_ab[...] = (slope + d_pre_b).astype(d_ab.dtype)
    d_small[0:1, :] += jnp.sum(d_decay * common["decay"], 0, keepdims=True)
    d_small[1:2, :] += jnp.sum(slope, 0, keepdims=True)
    d_gain[0:1, :] += gain_sum
    for store, ext, taps, d_taps, later, target in zip(
        (du_q, du_k, du_v), common["ext"], (taps_q, taps_k, taps_v), (d_taps_q, d_taps_k, d_taps_v),
        (next_q, next_k, next_v), (d_q, d_k, d_v),
    ):
        du = jnp.concatenate(store, 1) if heads > 1 else store[0]
        longer = jnp.concatenate([du, later[...]], 0)
        later[...] = du[0:8]
        total = taps[3:4, :] * du
        for offset in range(3):
            total = total + taps[offset : offset + 1, :] * longer[3 - offset : 3 - offset + block]
        target[...] = (total * valid).astype(target.dtype)
        for offset in range(4):
            d_taps[offset : offset + 1, :] += jnp.sum(du * ext[5 + offset : 5 + offset + block], 0, keepdims=True)


def input_specs(heads, block, place):
    wide_k, wide_v = heads * DK, heads * DV

    def tile(width):
        return pl.BlockSpec((None, block, width), lambda r, c, *_: (r, place(c), 0))

    def halo(width):
        return pl.BlockSpec(
            (None, 8, width), lambda r, c, *_: (r, jnp.maximum(place(c) * (block // 8) - 1, 0), 0))

    def fixed(rows, width):
        return pl.BlockSpec((rows, width), lambda r, c, *_: (0, 0))

    return [
        tile(wide_k), tile(wide_k), tile(wide_v), tile(wide_v), tile(LANES),
        halo(wide_k), halo(wide_k), halo(wide_v),
        fixed(8, wide_k), fixed(8, wide_k), fixed(8, wide_v),
        fixed(1, LANES), fixed(1, LANES), fixed(1, DV),
    ]


def operands(pre_q, pre_k, pre_v, pre_g, pre_ab, taps_q, taps_k, taps_v, rate, bias, gain):
    return (pre_q, pre_k, pre_v, pre_g, pre_ab, pre_q, pre_k, pre_v, taps_q, taps_k, taps_v, rate, bias, gain)


def mixer_forward(bounds, heads, block, *values):
    rows = values[0].shape[0]
    steps = SLOT // block
    wide_v = heads * DV
    tile_v = pl.BlockSpec((None, block, wide_v), lambda r, c, *_: (r, c, 0))
    return pl.pallas_call(
        functools.partial(forward_kernel, heads, block),
        grid_spec=pltpu.PrefetchScalarGridSpec(
            num_scalar_prefetch=1,
            grid=(rows, steps),
            in_specs=input_specs(heads, block, lambda c: c),
            out_specs=[
                tile_v, tile_v,
                pl.BlockSpec((None, None, heads, DK, DV), lambda r, c, *_: (r, c, 0, 0, 0)),
                tile_v,
                pl.BlockSpec((None, None, heads, block, block), lambda r, c, *_: (r, c, 0, 0, 0)),
            ],
            scratch_shapes=[pltpu.VMEM((heads, DK, DV), F32)],
        ),
        out_shape=[
            jax.ShapeDtypeStruct((rows, SLOT, wide_v), BF16),
            jax.ShapeDtypeStruct((rows, SLOT, wide_v), F32),
            jax.ShapeDtypeStruct((rows, steps, heads, DK, DV), F32),
            jax.ShapeDtypeStruct((rows, SLOT, wide_v), F32),
            jax.ShapeDtypeStruct((rows, steps, heads, block, block), F32),
        ],
        name="mixer_forward",
    )(bounds, *operands(*values))


def mixer_backward(bounds, heads, block, values, saved, grad):
    rows = values[0].shape[0]
    steps = SLOT // block
    wide_k, wide_v = heads * DK, heads * DV

    def tile(width):
        return pl.BlockSpec((None, block, width), lambda r, c, *_: (r, steps - 1 - c, 0))

    def fixed(rows, width):
        return pl.BlockSpec((rows, width), lambda r, c, *_: (0, 0))

    out, states, deltas, solves = saved
    return pl.pallas_call(
        functools.partial(backward_kernel, heads, block, steps),
        grid_spec=pltpu.PrefetchScalarGridSpec(
            num_scalar_prefetch=1,
            grid=(rows, steps),
            in_specs=input_specs(heads, block, lambda c: steps - 1 - c) + [
                tile(wide_v),
                pl.BlockSpec((None, None, heads, DK, DV), lambda r, c, *_: (r, steps - 1 - c, 0, 0, 0)),
                tile(wide_v),
                pl.BlockSpec((None, None, heads, block, block), lambda r, c, *_: (r, steps - 1 - c, 0, 0, 0)),
                tile(wide_v),
            ],
            out_specs=[
                tile(wide_k), tile(wide_k), tile(wide_v), tile(wide_v), tile(LANES),
                fixed(8, wide_k), fixed(8, wide_k), fixed(8, wide_v), fixed(8, LANES), fixed(8, DV),
            ],
            scratch_shapes=[
                pltpu.VMEM((heads, DK, DV), F32),
                pltpu.VMEM((8, wide_k), F32), pltpu.VMEM((8, wide_k), F32), pltpu.VMEM((8, wide_v), F32),
            ],
        ),
        out_shape=[
            jax.ShapeDtypeStruct((rows, SLOT, wide_k), BF16),
            jax.ShapeDtypeStruct((rows, SLOT, wide_k), BF16),
            jax.ShapeDtypeStruct((rows, SLOT, wide_v), BF16),
            jax.ShapeDtypeStruct((rows, SLOT, wide_v), BF16),
            jax.ShapeDtypeStruct((rows, SLOT, LANES), BF16),
            jax.ShapeDtypeStruct((8, wide_k), F32),
            jax.ShapeDtypeStruct((8, wide_k), F32),
            jax.ShapeDtypeStruct((8, wide_v), F32),
            jax.ShapeDtypeStruct((8, LANES), F32),
            jax.ShapeDtypeStruct((8, DV), F32),
        ],
        name="mixer_backward",
    )(bounds, *operands(*values), out, states, deltas, solves, grad)


def inner_rows(left, right):
    return lax.dot_general(
        left, right, (((0,), (0,)), ((), ())), preferred_element_type=jnp.float32
    )


def times_transposed(left, right):
    return lax.dot_general(
        left, right, (((1,), (1,)), ((), ())), preferred_element_type=jnp.float32
    )


def norm_backward(grad_normed, inputs, scale, gain):
    unit = inputs * scale
    weighted = grad_normed * gain
    grad_gain = jnp.sum(grad_normed * unit, 0)
    grad_inputs = scale * (weighted - unit * jnp.mean(weighted * unit, -1, keepdims=True))
    return (grad_inputs, grad_gain)


def shards(
    tokens,
    lengths,
    starts,
    norm_one,
    w_query,
    w_key,
    w_value,
    w_gating,
    w_decay,
    w_strength,
    filter_query,
    filter_key,
    filter_value,
    decay_log,
    decay_bias,
    head_gain,
    w_output,
    norm_two,
    w_gate,
    w_up,
    w_down,
    cotangent,
):
    rank = lax.axis_index("tensor")
    tok_dev = tokens.shape[0]
    rows = lengths.shape[0]
    heads_local = w_decay.shape[1]
    slot_pos = jnp.arange(SLOT, dtype=jnp.int32)
    row_mask = (
        (slot_pos[None, :] >= starts[:, None]) & (slot_pos[None, :] < (starts + lengths)[:, None])
    ).astype(jnp.float32)
    local_mask = lax.dynamic_slice_in_dim(row_mask.reshape(-1), rank * tok_dev, tok_dev)[:, None]
    gathered = (
        lax.all_gather(w_query, "dp", axis=0, tiled=True),
        lax.all_gather(w_key, "dp", axis=0, tiled=True),
        lax.all_gather(w_value, "dp", axis=0, tiled=True),
        lax.all_gather(w_gating, "dp", axis=0, tiled=True),
        lax.all_gather(w_decay, "dp", axis=0, tiled=True),
        lax.all_gather(w_strength, "dp", axis=0, tiled=True),
        lax.all_gather(w_output, "dp", axis=1, tiled=True),
        lax.all_gather(w_gate, "dp", axis=0, tiled=True),
        lax.all_gather(w_up, "dp", axis=0, tiled=True),
        lax.all_gather(w_down, "dp", axis=1, tiled=True),
    )
    (
        full_query,
        full_key,
        full_value,
        full_gating,
        full_decay,
        full_strength,
        full_output,
        full_gate,
        full_up,
        full_down,
    ) = gathered
    inputs = tokens.astype(jnp.float32)
    scale_one = lax.rsqrt(jnp.mean(inputs * inputs, -1, keepdims=True) + 1e-05)
    normed_one = (inputs * scale_one * norm_one).astype(jnp.bfloat16)
    rows_one = lax.all_gather(normed_one, "tensor", axis=0, tiled=True)
    projections = tuple(
        (
            jnp.dot(rows_one, weight, preferred_element_type=jnp.float32).reshape(rows, SLOT, -1)
            for weight in (full_query, full_key, full_value, full_gating, full_decay, full_strength)
        )
    )
    key_width = heads_local * DK
    value_width = heads_local * DV
    local_params = (
        lax.dynamic_slice_in_dim(filter_query, rank * key_width, key_width, 1),
        lax.dynamic_slice_in_dim(filter_key, rank * key_width, key_width, 1),
        lax.dynamic_slice_in_dim(filter_value, rank * value_width, value_width, 1),
        lax.dynamic_slice_in_dim(decay_log, rank * heads_local, heads_local),
        lax.dynamic_slice_in_dim(decay_bias, rank * heads_local, heads_local),
        head_gain,
    )

    local_q, local_k, local_v, local_log, local_bias, _ = local_params
    pad = LANES - 2 * heads_local
    both = jnp.pad(jnp.concatenate(projections[4:6], -1), ((0, 0), (0, 0), (0, pad)))
    rate = jnp.pad(-jnp.exp(local_log), (0, LANES - heads_local))[None]
    bias = jnp.pad(local_bias, (0, LANES - heads_local))[None]
    taps = tuple(jnp.pad(t, ((0, 4), (0, 0))) for t in (local_q, local_k, local_v))
    bounds = jnp.stack([starts, starts + lengths])
    values = projections[:4] + (both,) + taps + (rate, bias, head_gain[None])
    mixed_float, *saved = mixer_forward(bounds, heads_local, BLOCK, *values)
    mixed = mixed_float.reshape(rows * SLOT, -1).astype(jnp.bfloat16)
    attention = lax.psum_scatter(
        jnp.dot(mixed, full_output, preferred_element_type=jnp.float32),
        "tensor",
        scatter_dimension=0,
        tiled=True,
    )
    middle = inputs + attention
    scale_two = lax.rsqrt(jnp.mean(middle * middle, -1, keepdims=True) + 1e-05)
    normed_two = (middle * scale_two * norm_two).astype(jnp.bfloat16)
    rows_two = lax.all_gather(normed_two, "tensor", axis=0, tiled=True)
    gate_pre = jnp.dot(rows_two, full_gate, preferred_element_type=jnp.float32)
    up_pre = jnp.dot(rows_two, full_up, preferred_element_type=jnp.float32)
    hidden = (jax.nn.silu(gate_pre) * up_pre).astype(jnp.bfloat16)
    feed = lax.psum_scatter(
        jnp.dot(hidden, full_down, preferred_element_type=jnp.float32).astype(jnp.bfloat16),
        "tensor",
        scatter_dimension=0,
        tiled=True,
    ).astype(jnp.float32)
    block_out = (local_mask * (middle + feed)).astype(jnp.bfloat16)
    back_weights = (
        lax.all_gather(w_query, "dp", axis=0, tiled=True),
        lax.all_gather(w_key, "dp", axis=0, tiled=True),
        lax.all_gather(w_value, "dp", axis=0, tiled=True),
        lax.all_gather(w_gating, "dp", axis=0, tiled=True),
        lax.all_gather(w_decay, "dp", axis=0, tiled=True),
        lax.all_gather(w_strength, "dp", axis=0, tiled=True),
        lax.all_gather(w_output, "dp", axis=1, tiled=True),
        lax.all_gather(w_gate, "dp", axis=0, tiled=True),
        lax.all_gather(w_up, "dp", axis=0, tiled=True),
        lax.all_gather(w_down, "dp", axis=1, tiled=True),
    )
    (
        back_query,
        back_key,
        back_value,
        back_gating,
        back_decay,
        back_strength,
        back_output,
        back_gate,
        back_up,
        back_down,
    ) = back_weights
    residual_grad = cotangent.astype(jnp.float32) * local_mask
    feed_grad = lax.all_gather(residual_grad.astype(jnp.bfloat16), "tensor", axis=0, tiled=True)
    hidden_grad = times_transposed(feed_grad, back_down)
    grad_down = inner_rows(hidden, feed_grad)
    sigmoid_gate = jax.nn.sigmoid(gate_pre)
    gate_grad = (
        hidden_grad * up_pre * sigmoid_gate * (1.0 + gate_pre * (1.0 - sigmoid_gate))
    ).astype(jnp.bfloat16)
    up_grad = (hidden_grad * gate_pre * sigmoid_gate).astype(jnp.bfloat16)
    grad_gate = inner_rows(rows_two, gate_grad)
    grad_up = inner_rows(rows_two, up_grad)
    normed_two_grad = lax.psum_scatter(
        times_transposed(gate_grad, back_gate) + times_transposed(up_grad, back_up),
        "tensor",
        scatter_dimension=0,
        tiled=True,
    )
    middle_part, grad_norm_two = norm_backward(normed_two_grad, middle, scale_two, norm_two)
    middle_grad = residual_grad + middle_part
    attention_grad = lax.all_gather(middle_grad.astype(jnp.bfloat16), "tensor", axis=0, tiled=True)
    mixed_grad = times_transposed(attention_grad, back_output)
    grad_output = inner_rows(mixed, attention_grad)
    g = mixer_backward(
        bounds, heads_local, BLOCK, values, saved, mixed_grad.reshape(rows, SLOT, -1)
    )
    both_grad = g[4][..., :heads_local], g[4][..., heads_local : 2 * heads_local]
    pulled = tuple(g[:4]) + both_grad + (
        g[5][:4], g[6][:4], g[7][:4], g[8][0, :heads_local], g[8][1, :heads_local], g[9][0]
    )
    projection_grads = tuple(
        (grad.reshape(rows * SLOT, -1).astype(jnp.bfloat16) for grad in pulled[:6])
    )
    weight_grads = tuple((inner_rows(rows_one, grad) for grad in projection_grads))
    back_projections = (back_query, back_key, back_value, back_gating, back_decay, back_strength)
    normed_one_part = times_transposed(projection_grads[0], back_projections[0])
    for grad, weight in zip(projection_grads[1:], back_projections[1:]):
        normed_one_part = normed_one_part + times_transposed(grad, weight)
    normed_one_grad = lax.psum_scatter(
        normed_one_part.astype(jnp.bfloat16), "tensor", scatter_dimension=0, tiled=True
    ).astype(jnp.float32)
    input_part, grad_norm_one = norm_backward(normed_one_grad, inputs, scale_one, norm_one)
    grad_tokens = middle_grad + input_part
    placed_query = lax.dynamic_update_slice_in_dim(
        jnp.zeros_like(filter_query), pulled[6], rank * key_width, 1
    )
    placed_key = lax.dynamic_update_slice_in_dim(
        jnp.zeros_like(filter_key), pulled[7], rank * key_width, 1
    )
    placed_value = lax.dynamic_update_slice_in_dim(
        jnp.zeros_like(filter_value), pulled[8], rank * value_width, 1
    )
    placed_log = lax.dynamic_update_slice_in_dim(
        jnp.zeros_like(decay_log), pulled[9], rank * heads_local, 0
    )
    placed_bias = lax.dynamic_update_slice_in_dim(
        jnp.zeros_like(decay_bias), pulled[10], rank * heads_local, 0
    )
    summed = lax.psum(
        (
            grad_norm_one,
            grad_norm_two,
            pulled[11],
            placed_query,
            placed_key,
            placed_value,
            placed_log,
            placed_bias,
        ),
        ("dp", "tensor"),
    )
    (
        sum_norm_one,
        sum_norm_two,
        sum_head_gain,
        sum_filter_query,
        sum_filter_key,
        sum_filter_value,
        sum_decay_log,
        sum_decay_bias,
    ) = summed
    (
        owned_query,
        owned_key,
        owned_value,
        owned_gating,
        owned_decay,
        owned_strength,
        owned_output,
        owned_gate,
        owned_up,
        owned_down,
    ) = (
        lax.psum_scatter(weight_grads[0], "dp", scatter_dimension=0, tiled=True),
        lax.psum_scatter(weight_grads[1], "dp", scatter_dimension=0, tiled=True),
        lax.psum_scatter(weight_grads[2], "dp", scatter_dimension=0, tiled=True),
        lax.psum_scatter(weight_grads[3], "dp", scatter_dimension=0, tiled=True),
        lax.psum_scatter(weight_grads[4], "dp", scatter_dimension=0, tiled=True),
        lax.psum_scatter(weight_grads[5], "dp", scatter_dimension=0, tiled=True),
        lax.psum_scatter(grad_output, "dp", scatter_dimension=1, tiled=True),
        lax.psum_scatter(grad_gate, "dp", scatter_dimension=0, tiled=True),
        lax.psum_scatter(grad_up, "dp", scatter_dimension=0, tiled=True),
        lax.psum_scatter(grad_down, "dp", scatter_dimension=1, tiled=True),
    )
    return (
        block_out,
        grad_tokens,
        sum_norm_one,
        owned_query,
        owned_key,
        owned_value,
        owned_gating,
        owned_decay,
        owned_strength,
        sum_filter_query,
        sum_filter_key,
        sum_filter_value,
        sum_decay_log,
        sum_decay_bias,
        sum_head_gain,
        owned_output,
        sum_norm_two,
        owned_gate,
        owned_up,
        owned_down,
    )


def solution(mesh):
    placed = (
        P(("dp", "tensor"), None),
        P("dp"),
        P("dp"),
        P(),
        P("dp", "tensor"),
        P("dp", "tensor"),
        P("dp", "tensor"),
        P("dp", "tensor"),
        P("dp", "tensor"),
        P("dp", "tensor"),
        P(),
        P(),
        P(),
        P(),
        P(),
        P(),
        P("tensor", "dp"),
        P(),
        P("dp", "tensor"),
        P("dp", "tensor"),
        P("tensor", "dp"),
        P(("dp", "tensor"), None),
    )
    return jax.shard_map(
        shards,
        mesh=mesh,
        in_specs=placed,
        out_specs=(
            P(("dp", "tensor"), None),
            P(("dp", "tensor"), None),
            P(),
            P("dp", "tensor"),
            P("dp", "tensor"),
            P("dp", "tensor"),
            P("dp", "tensor"),
            P("dp", "tensor"),
            P("dp", "tensor"),
            P(),
            P(),
            P(),
            P(),
            P(),
            P(),
            P("tensor", "dp"),
            P(),
            P("dp", "tensor"),
            P("dp", "tensor"),
            P("tensor", "dp"),
        ),
        check_vma=False,
    )
```

```python
import functools
import jax
import jax.numpy as jnp
from jax import lax
from jax.experimental import pallas as pl
from jax.experimental.pallas import tpu as pltpu
from jax.sharding import PartitionSpec as P

DK = 128
DV = 256
SLOT = 1024
LANES = 128
BLOCK = 256
HEADS = 2
WIDE_K = HEADS * DK
WIDE_V = HEADS * DV
WIDTH = 2 * WIDE_K + 2 * WIDE_V + LANES
F32 = jnp.float32
BF16 = jnp.bfloat16


def dot(left, right, dim_left, dim_right):
    return lax.dot_general(
        left, right, (((dim_left,), (dim_right,)), ((), ())), preferred_element_type=F32
    )


def halves(value):
    high = value.astype(BF16)
    return high, (value - high.astype(F32)).astype(BF16)


def mm(left, right, dim_left=1, dim_right=0):
    left_high, left_low = halves(left)
    right_high, right_low = halves(right)
    return (
        dot(left_high, right_high, dim_left, dim_right)
        + dot(left_high, right_low, dim_left, dim_right)
        + dot(left_low, right_high, dim_left, dim_right)
    )


def mm_full(left, right, dim_left, dim_right):
    return lax.dot_general(
        left,
        right,
        (((dim_left,), (dim_right,)), ((), ())),
        preferred_element_type=F32,
        precision=lax.Precision.HIGHEST,
    )


def sigmoid(value):
    return 1.0 / (1.0 + jnp.exp(-value))


def softplus(value):
    return jnp.maximum(value, 0.0) + jnp.log1p(jnp.exp(-jnp.abs(value)))


def valid_rows(first, count, start, end):
    position = first + lax.broadcasted_iota(jnp.int32, (count, 1), 0)
    return jnp.where((position >= start) & (position < end), 1.0, 0.0).astype(F32)


def convolve(extended, taps, count):
    total = taps[0:1, :] * extended[5 : 5 + count]
    for offset in range(1, 4):
        total = total + taps[offset : offset + 1, :] * extended[5 + offset : 5 + offset + count]
    return total


def unit_scale(value):
    return lax.rsqrt(jnp.sum(value * value, -1, keepdims=True) + 1e-06)


def triangle(size):
    row = lax.broadcasted_iota(jnp.int32, (size, size), 0)
    column = lax.broadcasted_iota(jnp.int32, (size, size), 1)
    return row, column


def lower_ones(size):
    row, column = triangle(size)
    return jnp.where(row >= column, 1.0, 0.0).astype(F32)


def inverses(systems, size):
    row, column = triangle(size)
    differ = jnp.bitwise_xor(row, column)
    eye = jnp.where(differ == 0, 1.0, 0.0).astype(F32)
    found = [eye - jnp.where(differ == 1, system, 0.0) for system in systems]
    width = 2
    while width < size:
        mask = (differ >= width) & (differ < 2 * width)
        parts = [jnp.where(mask, system, 0.0) for system in systems]
        middle = [mm(f, p) for f, p in zip(found, parts)]
        found = [f - mm(m, f) for f, m in zip(found, middle)]
        width *= 2
    return found


def gather_inputs(first, start, end, refs, heads, block):
    pre_q, pre_k, pre_v, pre_ab, halo_q, halo_k, halo_v, taps_q, taps_k, taps_v, rate, bias = refs
    valid = valid_rows(first, block, start, end)
    halo_valid = valid_rows(first - 8, 8, start, end)
    ext_q = jnp.concatenate([halo_q[...] * halo_valid, pre_q[...] * valid], 0)
    ext_k = jnp.concatenate([halo_k[...] * halo_valid, pre_k[...] * valid], 0)
    ext_v = jnp.concatenate([halo_v[...] * halo_valid, pre_v[...] * valid], 0)
    conv_q = convolve(ext_q, taps_q[...], block)
    conv_k = convolve(ext_k, taps_k[...], block)
    conv_v = convolve(ext_v, taps_v[...], block)
    both = pre_ab[...]
    shifted = both + bias[...]
    decay = rate[...] * softplus(shifted) * valid
    strength = sigmoid(both) * valid
    ones = lower_ones(block)
    cum = mm_full(ones, decay, 1, 0)
    cum_rows = mm_full(decay, ones, 0, 1)
    return dict(
        valid=valid, ext=(ext_q, ext_k, ext_v), conv=(conv_q, conv_k, conv_v), shifted=shifted,
        decay=decay, strength=strength, ones=ones, cum=cum, cum_rows=cum_rows,
    )


def head_operands(common, head, heads, block):
    conv_q, conv_k, conv_v = common["conv"]
    keys = slice(head * DK, (head + 1) * DK)
    vals = slice(head * DV, (head + 1) * DV)
    u_q, u_k, u_v = conv_q[:, keys], conv_k[:, keys], conv_v[:, vals]
    s_q, s_k, s_v = sigmoid(u_q), sigmoid(u_k), sigmoid(u_v)
    y_q, y_k = u_q * s_q, u_k * s_k
    n_q, n_k = unit_scale(y_q), unit_scale(y_k)
    cum = common["cum"][:, head : head + 1]
    cum_row = common["cum_rows"][head : head + 1, :]
    last = common["cum"][block - 1 : block, head : head + 1]
    spread = jnp.exp(jnp.minimum(cum - cum_row, 0.0))
    return dict(
        u=(u_q, u_k, u_v), s=(s_q, s_k, s_v), n=(n_q, n_k), unit=(y_q * n_q, y_k * n_k),
        q=y_q * (n_q * DK ** (-0.5)), k=y_k * (n_k * common["valid"]), v=u_v * s_v,
        beta=common["strength"][:, heads + head : heads + head + 1],
        growth=jnp.exp(cum), remain=jnp.exp(last - cum), whole=jnp.exp(last), spread=spread,
    )


def forward_kernel(heads, block, bounds, pre_q, pre_k, pre_v, pre_g, pre_ab, halo_q, halo_k, halo_v,
                   taps_q, taps_k, taps_v, rate, bias, gain, mixed, out, states, deltas, solves, state):
    row, step = pl.program_id(0), pl.program_id(1)

    @pl.when(step == 0)
    def _():
        state[...] = jnp.zeros_like(state)

    refs = (pre_q, pre_k, pre_v, pre_ab, halo_q, halo_k, halo_v, taps_q, taps_k, taps_v, rate, bias)
    common = gather_inputs(step * block, bounds[0, row], bounds[1, row], refs, heads, block)
    ops = [head_operands(common, head, heads, block) for head in range(heads)]
    at, to = triangle(block)
    systems = [jnp.where(at > to, o["beta"] * o["spread"] * mm(o["k"], o["k"], 1, 1), 0.0) for o in ops]
    found = inverses(systems, block)
    for head, o in enumerate(ops):
        vals = slice(head * DV, (head + 1) * DV)
        old = state[head]
        states[head] = old.astype(states.dtype)
        source = o["beta"] * o["v"] - (o["beta"] * o["growth"]) * mm(o["k"], old)
        delta = mm(found[head], source)
        scores = jnp.where(at >= to, o["spread"] * mm(o["q"], o["k"], 1, 1), 0.0)
        emitted = o["growth"] * mm(o["q"], old) + mm(scores, delta)
        state[head] = o["whole"] * old + mm(o["k"] * o["remain"], delta, 0, 0)
        solves[head] = found[head].astype(solves.dtype)
        deltas[:, vals] = delta.astype(deltas.dtype)
        out[:, vals] = emitted.astype(out.dtype)
        scale = lax.rsqrt(jnp.mean(emitted * emitted, -1, keepdims=True) + 1e-05)
        gate = pre_g[:, vals]
        mixed[:, vals] = (
            emitted * scale * gain[...] * (gate * sigmoid(gate)) * common["valid"]
        ).astype(mixed.dtype)


def backward_kernel(heads, block, steps, bounds, pre_q, pre_k, pre_v, pre_g, pre_ab, halo_q, halo_k, halo_v,
                    taps_q, taps_k, taps_v, rate, bias, gain, out, states, deltas, solves, grad,
                    d_pre, d_taps_q, d_taps_k, d_taps_v, d_small, d_gain,
                    d_state, next_q, next_k, next_v):
    d_q = d_pre.at[:, 0:WIDE_K]
    d_k = d_pre.at[:, WIDE_K : 2 * WIDE_K]
    d_v = d_pre.at[:, 2 * WIDE_K : 2 * WIDE_K + WIDE_V]
    d_g = d_pre.at[:, 2 * WIDE_K + WIDE_V : 2 * WIDE_K + 2 * WIDE_V]
    d_ab = d_pre.at[:, 2 * WIDE_K + 2 * WIDE_V : WIDTH]
    row, back = pl.program_id(0), pl.program_id(1)
    step = steps - 1 - back

    @pl.when((row == 0) & (back == 0))
    def _():
        for ref in (d_taps_q, d_taps_k, d_taps_v, d_small, d_gain):
            ref[...] = jnp.zeros_like(ref)

    @pl.when(back == 0)
    def _():
        for ref in (d_state, next_q, next_k, next_v):
            ref[...] = jnp.zeros_like(ref)

    refs = (pre_q, pre_k, pre_v, pre_ab, halo_q, halo_k, halo_v, taps_q, taps_k, taps_v, rate, bias)
    common = gather_inputs(step * block, bounds[0, row], bounds[1, row], refs, heads, block)
    valid = common["valid"]
    at, to = triangle(block)
    lane = lax.broadcasted_iota(jnp.int32, (block, LANES), 1)
    ones_cols = jnp.ones((block, LANES), BF16)
    d_cum = jnp.zeros((block, LANES), F32)
    d_last = jnp.zeros((1, LANES), F32)
    d_beta = jnp.zeros((block, LANES), F32)
    du_q, du_k, du_v = [], [], []
    gain_sum = jnp.zeros((1, DV), F32)
    for head in range(heads):
        o = head_operands(common, head, heads, block)
        vals = slice(head * DV, (head + 1) * DV)
        q, k, v, beta, growth, remain, whole, spread = (
            o[name] for name in ("q", "k", "v", "beta", "growth", "remain", "whole", "spread"))
        emitted = out[:, vals].astype(F32)
        scale = lax.rsqrt(jnp.mean(emitted * emitted, -1, keepdims=True) + 1e-05)
        unit = emitted * scale
        gate = pre_g[:, vals]
        s_g = sigmoid(gate)
        d_mixed = grad[:, vals].astype(F32) * valid
        d_g[:, vals] = (d_mixed * unit * gain[...] * (s_g * (1.0 + gate * (1.0 - s_g)))).astype(d_g.dtype)
        part = d_mixed * (gate * s_g)
        gain_sum = gain_sum + jnp.sum(part * unit, 0, keepdims=True)
        weighted = part * gain[...]
        d_out = scale * (weighted - unit * jnp.mean(weighted * unit, -1, keepdims=True))
        old = states[head].astype(F32)
        delta = deltas[:, vals]
        solve = solves[head]
        d_new = d_state[head]
        q_k = mm(q, k, 1, 1)
        k_k = mm(k, k, 1, 1)
        scores = jnp.where(at >= to, spread * q_k, 0.0)
        linked = jnp.where(at > to, spread * k_k, 0.0)
        k_s = mm(k, old)
        q_s = mm(q, old)
        k_rem = k * remain
        d_delta = mm(scores, d_out, 0, 0) + mm(k_rem, d_new)
        d_source = mm(solve, d_delta, 0, 0)
        d_system = -mm(d_source, delta, 1, 1)
        d_scores = mm(d_out, delta, 1, 1)
        d_qk = jnp.where(at >= to, d_scores * spread, 0.0)
        by_link = d_system * linked
        d_kk = jnp.where(at > to, beta * d_system * spread, 0.0)
        edge, edge_low = halves(d_scores * scores + beta * by_link)
        d_query = growth * mm(d_out, old, 1, 1) + mm(d_qk, k)
        back_state = mm(delta, d_new, 1, 1)
        d_key = (
            mm((beta * growth) * d_source, old, 1, 1) * (-1.0)
            + mm(d_qk, q, 0, 0)
            + mm(d_kk, k)
            + mm(d_kk, k, 0, 0)
            + remain * back_state
        )
        d_value = beta * d_source
        lose = jnp.sum(k_rem * back_state, -1, keepdims=True)
        pull = jnp.sum(d_source * k_s, -1, keepdims=True)
        grow = growth * (jnp.sum(d_out * q_s, -1, keepdims=True) - beta * pull)
        d_b = jnp.sum(d_source * v, -1, keepdims=True) - growth * pull + jnp.sum(by_link, -1, keepdims=True)
        cut = (
            dot(edge, ones_cols, 1, 0) - dot(edge, ones_cols, 0, 0)
            + dot(edge_low, ones_cols, 1, 0) - dot(edge_low, ones_cols, 0, 0)
        )
        d_cum = jnp.where(lane == head, cut + (grow - lose), d_cum)
        d_beta = jnp.where(lane == heads + head, d_b, d_beta)
        total = jnp.sum(lose, keepdims=True) + whole * jnp.sum(old * d_new, keepdims=True)
        d_last = jnp.where(lane[0:1] == head, total, d_last)
        d_state[head] = (
            whole * d_new + mm(q, growth * d_out, 0, 0) - mm(k * (beta * growth), d_source, 0, 0)
        )
        unit_q, unit_k = o["unit"]
        n_q, n_k = o["n"]
        d_unit = d_query * DK ** (-0.5)
        d_yq = n_q * (d_unit - unit_q * jnp.sum(unit_q * d_unit, -1, keepdims=True))
        d_unit = d_key * valid
        d_yk = n_k * (d_unit - unit_k * jnp.sum(unit_k * d_unit, -1, keepdims=True))
        for store, d_y, u, s in zip((du_q, du_k, du_v), (d_yq, d_yk, d_value), o["u"], o["s"]):
            store.append(d_y * (s * (1.0 + u * (1.0 - s))))
    d_decay = mm_full(common["ones"], d_cum, 0, 0) + d_last
    slope = d_decay * rate[...] * sigmoid(common["shifted"]) * valid
    strength = common["strength"]
    d_pre_b = d_beta * strength * (1.0 - strength)
    d_ab[...] = (slope + d_pre_b).astype(d_ab.dtype)
    d_small[0:1, :] += jnp.sum(d_decay * common["decay"], 0, keepdims=True)
    d_small[1:2, :] += jnp.sum(slope, 0, keepdims=True)
    d_gain[0:1, :] += gain_sum
    for store, ext, taps, d_taps, later, target in zip(
        (du_q, du_k, du_v), common["ext"], (taps_q, taps_k, taps_v), (d_taps_q, d_taps_k, d_taps_v),
        (next_q, next_k, next_v), (d_q, d_k, d_v),
    ):
        du = jnp.concatenate(store, 1) if heads > 1 else store[0]
        longer = jnp.concatenate([du, later[...]], 0)
        later[...] = du[0:8]
        total = taps[3:4, :] * du
        for offset in range(3):
            total = total + taps[offset : offset + 1, :] * longer[3 - offset : 3 - offset + block]
        target[...] = (total * valid).astype(target.dtype)
        for offset in range(4):
            d_taps[offset : offset + 1, :] += jnp.sum(du * ext[5 + offset : 5 + offset + block], 0, keepdims=True)


def pre_specs(place):
    def tile(width, column):
        return pl.BlockSpec((None, BLOCK, width), lambda r, c, *_: (r, place(c), column))

    def halo(width, column):
        return pl.BlockSpec(
            (None, 8, width),
            lambda r, c, *_: (r, jnp.maximum(place(c) * (BLOCK // 8) - 1, 0), column),
        )

    def fixed(rows, width):
        return pl.BlockSpec((rows, width), lambda r, c, *_: (0, 0))

    return [
        tile(WIDE_K, 0), tile(WIDE_K, 1), tile(WIDE_V, 1), tile(WIDE_V, 2),
        tile(LANES, (WIDTH - LANES) // LANES),
        halo(WIDE_K, 0), halo(WIDE_K, 1), halo(WIDE_V, 1),
        fixed(8, WIDE_K), fixed(8, WIDE_K), fixed(8, WIDE_V),
        fixed(1, LANES), fixed(1, LANES), fixed(1, DV),
    ]


def mixer_forward(bounds, pre, small):
    rows = pre.shape[0]
    steps = SLOT // BLOCK
    tile_v = pl.BlockSpec((None, BLOCK, WIDE_V), lambda r, c, *_: (r, c, 0))
    return pl.pallas_call(
        functools.partial(forward_kernel, HEADS, BLOCK),
        grid_spec=pltpu.PrefetchScalarGridSpec(
            num_scalar_prefetch=1,
            grid=(rows, steps),
            in_specs=pre_specs(lambda c: c),
            out_specs=[
                tile_v, tile_v,
                pl.BlockSpec((None, None, HEADS, DK, DV), lambda r, c, *_: (r, c, 0, 0, 0)),
                tile_v,
                pl.BlockSpec((None, None, HEADS, BLOCK, BLOCK), lambda r, c, *_: (r, c, 0, 0, 0)),
            ],
            scratch_shapes=[pltpu.VMEM((HEADS, DK, DV), F32)],
        ),
        out_shape=[
            jax.ShapeDtypeStruct((rows, SLOT, WIDE_V), BF16),
            jax.ShapeDtypeStruct((rows, SLOT, WIDE_V), F32),
            jax.ShapeDtypeStruct((rows, steps, HEADS, DK, DV), F32),
            jax.ShapeDtypeStruct((rows, SLOT, WIDE_V), F32),
            jax.ShapeDtypeStruct((rows, steps, HEADS, BLOCK, BLOCK), F32),
        ],
        cost_estimate=pl.CostEstimate(
            flops=10**10 * rows, bytes_accessed=2 * 10**7 * rows, transcendentals=10**7 * rows),
        name="mixer_forward",
    )(bounds, *[pre] * 8, *small)


def mixer_backward(bounds, pre, small, saved, grad):
    rows = pre.shape[0]
    steps = SLOT // BLOCK

    def tile(width):
        return pl.BlockSpec((None, BLOCK, width), lambda r, c, *_: (r, steps - 1 - c, 0))

    def fixed(rows, width):
        return pl.BlockSpec((rows, width), lambda r, c, *_: (0, 0))

    return pl.pallas_call(
        functools.partial(backward_kernel, HEADS, BLOCK, steps),
        grid_spec=pltpu.PrefetchScalarGridSpec(
            num_scalar_prefetch=1,
            grid=(rows, steps),
            in_specs=pre_specs(lambda c: steps - 1 - c) + [
                tile(WIDE_V),
                pl.BlockSpec((None, None, HEADS, DK, DV), lambda r, c, *_: (r, steps - 1 - c, 0, 0, 0)),
                tile(WIDE_V),
                pl.BlockSpec((None, None, HEADS, BLOCK, BLOCK), lambda r, c, *_: (r, steps - 1 - c, 0, 0, 0)),
                tile(WIDE_V),
            ],
            out_specs=[
                tile(WIDTH),
                fixed(8, WIDE_K), fixed(8, WIDE_K), fixed(8, WIDE_V), fixed(8, LANES), fixed(8, DV),
            ],
            scratch_shapes=[
                pltpu.VMEM((HEADS, DK, DV), F32),
                pltpu.VMEM((8, WIDE_K), F32), pltpu.VMEM((8, WIDE_K), F32), pltpu.VMEM((8, WIDE_V), F32),
            ],
        ),
        out_shape=[
            jax.ShapeDtypeStruct((rows, SLOT, WIDTH), BF16),
            jax.ShapeDtypeStruct((8, WIDE_K), F32),
            jax.ShapeDtypeStruct((8, WIDE_K), F32),
            jax.ShapeDtypeStruct((8, WIDE_V), F32),
            jax.ShapeDtypeStruct((8, LANES), F32),
            jax.ShapeDtypeStruct((8, DV), F32),
        ],
        cost_estimate=pl.CostEstimate(
            flops=10**10 * rows, bytes_accessed=2 * 10**7 * rows, transcendentals=10**7 * rows),
        name="mixer_backward",
    )(bounds, *[pre] * 8, *small, *saved, grad)


def matmul(left, right):
    return jnp.dot(left, right, preferred_element_type=F32)


def matmul_t(left, right):
    return lax.dot_general(left, right, (((1,), (1,)), ((), ())), preferred_element_type=F32)


def inner(left, right):
    return lax.dot_general(left, right, (((0,), (0,)), ((), ())), preferred_element_type=F32)


def norm_backward(grad_normed, inputs, scale, gain):
    unit = inputs * scale
    weighted = grad_normed * gain
    grad_gain = jnp.sum(grad_normed * unit, 0)
    grad_inputs = scale * (weighted - unit * jnp.mean(weighted * unit, -1, keepdims=True))
    return (grad_inputs, grad_gain)


def swap(value, axis, size, mask):
    return lax.ppermute(value, axis, [(i, i ^ mask) for i in range(size)])


def relative_order(devices):
    return list(range(0, devices, 2)) + list(range(1, devices, 2))


def relative_matrix(width, devices, me):
    block = width // devices
    order = jnp.array(relative_order(devices), jnp.int32)
    column = jnp.arange(width, dtype=jnp.int32)
    source = jnp.bitwise_xor(jnp.repeat(order, block), me) * block + column % block
    return (jnp.arange(width, dtype=jnp.int32)[:, None] == source[None, :]).astype(BF16)


def scatter_sum(product, left, devices):
    half = left.shape[1] // 2
    block = half * 2 // devices
    got = swap(product(left[:, half:]).astype(BF16), "dp", devices, 1)
    keep = product(left[:, :half]) + got.astype(F32)
    count, stride = devices // 2, 2
    lead = keep.shape[:-2]
    while count > 1:
        ways = min(4, count)
        shaped = keep.reshape(lead + (count // ways, ways, block, keep.shape[-1]))
        keep = shaped[..., :, 0, :, :]
        for way in range(1, ways):
            sent = shaped[..., :, way, :, :].astype(BF16)
            keep = keep + swap(sent, "dp", devices, way * stride).astype(F32)
        count //= ways
        stride *= ways
        keep = keep.reshape(lead + (count * block, keep.shape[-1]))
    return keep


def shards(
    tokens, lengths, starts, norm_one, w_query, w_key, w_value, w_gating, w_decay, w_strength,
    filter_query, filter_key, filter_value, decay_log, decay_bias, head_gain, w_output, norm_two,
    w_gate, w_up, w_down, cotangent,
):
    rank, me = lax.axis_index("tensor"), lax.axis_index("dp")
    ranks, devices = lax.axis_size("tensor"), lax.axis_size("dp")
    tok_dev, width = tokens.shape
    units = w_gate.shape[1]
    wide = -(-units // LANES) * LANES
    half = rank % 2
    row = rank // 2
    slot_pos = jnp.arange(SLOT, dtype=jnp.int32)
    row_mask = (
        (slot_pos[None, :] >= starts[:, None]) & (slot_pos[None, :] < (starts + lengths)[:, None])
    ).astype(F32)
    mask = lax.dynamic_slice_in_dim(row_mask.reshape(-1), rank * tok_dev, tok_dev)[:, None]
    bounds = lax.dynamic_slice_in_dim(jnp.stack([starts, starts + lengths]), row, 1, 1)

    def both_halves(mine, other):
        return jnp.where(half == 0, jnp.concatenate([mine, other], 0), jnp.concatenate([other, mine], 0))

    def exchange(value):
        return swap(value, "tensor", ranks, 1)

    inputs = tokens.astype(F32)
    scale_one = lax.rsqrt(jnp.mean(inputs * inputs, -1, keepdims=True) + 1e-05)
    normed_one = (inputs * scale_one * norm_one).astype(BF16)
    row_one = both_halves(normed_one, exchange(normed_one))

    spare = jnp.zeros((w_query.shape[0], LANES - 2 * HEADS), BF16)
    packed = jnp.concatenate([w_query, w_key, w_value, w_gating, w_decay, w_strength, spare], 1)
    first = lax.ppermute(packed, "tensor", [(1, 0), (3, 1), (2, 3), (0, 2)])
    second = lax.ppermute(packed, "tensor", [(1, 2), (2, 1)])
    lower = jnp.where(rank == 0, packed, jnp.where(rank == 1, second, first))
    upper = jnp.where(rank == 3, packed, jnp.where(rank == 2, second, first))
    mixer_weights = [lax.all_gather(w, "dp", axis=0, tiled=True) for w in (lower, upper)]

    def gather(value):
        whole = lax.all_gather(value, ("tensor", "dp"), axis=0, tiled=True)
        return whole.reshape(ranks, width, value.shape[1])

    pad = ((0, 0), (0, wide - units))
    out_t = gather(w_output.T)
    gate_w = gather(jnp.pad(w_gate, pad))
    up_w = gather(jnp.pad(w_up, pad))
    down_t = gather(jnp.pad(w_down.T, pad))

    def small_of(shard):
        def taps(values, columns):
            return jnp.pad(lax.dynamic_slice_in_dim(values, shard * columns, columns, 1), ((0, 4), (0, 0)))

        log = lax.dynamic_slice_in_dim(decay_log, shard * HEADS, HEADS)
        bias = lax.dynamic_slice_in_dim(decay_bias, shard * HEADS, HEADS)
        return (
            taps(filter_query, WIDE_K), taps(filter_key, WIDE_K), taps(filter_value, WIDE_V),
            jnp.pad(-jnp.exp(log), (0, LANES - HEADS))[None],
            jnp.pad(bias, (0, LANES - HEADS))[None],
            head_gain[None],
        )

    shard_ids = [2 * half, 2 * half + 1]
    smalls = [small_of(s) for s in shard_ids]
    pres = [matmul(row_one, w)[None] for w in mixer_weights]
    saves, own, got = [], [], []
    for pre, small in zip(pres, smalls):
        mixed, *saved = mixer_forward(bounds, pre, small)
        saves.append(saved)
        own.append(lax.dynamic_slice_in_dim(mixed[0], half * tok_dev, tok_dev))
        got.append(exchange(lax.dynamic_slice_in_dim(mixed[0], (1 - half) * tok_dev, tok_dev)))
    mixed = [jnp.where(half == 0, a, b) for a, b in zip(own + got, got + own)]
    attention = matmul_t(mixed[0], out_t[0])
    for part, weight in zip(mixed[1:], out_t[1:]):
        attention = attention + matmul_t(part, weight)
    middle = inputs + attention
    scale_two = lax.rsqrt(jnp.mean(middle * middle, -1, keepdims=True) + 1e-05)
    normed_two = (middle * scale_two * norm_two).astype(BF16)

    relative = relative_matrix(width, devices, me)

    def to_relative(value):
        return matmul(value, relative).astype(BF16)

    residual_grad = cotangent.astype(F32) * mask
    feed_grad = residual_grad.astype(BF16)
    feed_rel = to_relative(feed_grad)
    two_rel = to_relative(normed_two)
    feed = None
    two_grad = None
    hiddens, gate_grads, up_grads = [], [], []
    for t in range(ranks):
        gate_pre = matmul(normed_two, gate_w[t])
        up_pre = matmul(normed_two, up_w[t])
        s = jax.nn.sigmoid(gate_pre)
        hidden = (gate_pre * s * up_pre).astype(BF16)
        hidden_grad = matmul(feed_grad, down_t[t])
        gate_grad = (hidden_grad * up_pre * s * (1.0 + gate_pre * (1.0 - s))).astype(BF16)
        up_grad = (hidden_grad * gate_pre * s).astype(BF16)
        hiddens.append(hidden)
        gate_grads.append(gate_grad)
        up_grads.append(up_grad)
        part = matmul_t(hidden, down_t[t])
        feed = part if feed is None else feed + part
        part = matmul_t(gate_grad, gate_w[t]) + matmul_t(up_grad, up_w[t])
        two_grad = part if two_grad is None else two_grad + part
    block_out = (mask * (middle + feed)).astype(BF16)

    def many(values):
        return lambda left: jnp.stack([inner(left, v) for v in values])

    sum_gate = scatter_sum(many(gate_grads), two_rel, devices)
    sum_up = scatter_sum(many(up_grads), two_rel, devices)
    sum_down = scatter_sum(many(hiddens), feed_rel, devices)

    middle_part, grad_norm_two = norm_backward(two_grad, middle, scale_two, norm_two)
    middle_grad = residual_grad + middle_part
    attention_grad = middle_grad.astype(BF16)
    mixed_grads = []
    for j in range(2):
        sent = matmul(attention_grad, out_t[2 * (1 - half) + j]).astype(BF16)
        kept = matmul(attention_grad, out_t[2 * half + j]).astype(BF16)
        mixed_grads.append(both_halves(kept, exchange(sent))[None])
    sum_out = scatter_sum(many(mixed), to_relative(attention_grad), devices)

    one_rel = to_relative(row_one)
    one_part = None
    mixer_sums, smalls_grads = [], []
    for j in range(2):
        d_pre, *d_small = mixer_backward(bounds, pres[j], smalls[j], saves[j], mixed_grads[j])
        d_pre = d_pre[0]
        smalls_grads.append(d_small)
        mixer_sums.append(scatter_sum(lambda left: inner(left, d_pre), one_rel, devices))
        part = matmul_t(d_pre, mixer_weights[j])
        one_part = part if one_part is None else one_part + part
    one_kept = lax.dynamic_slice_in_dim(one_part, half * tok_dev, tok_dev)
    one_sent = lax.dynamic_slice_in_dim(one_part, (1 - half) * tok_dev, tok_dev)
    one_grad = one_kept + exchange(one_sent.astype(BF16)).astype(F32)
    input_part, grad_norm_one = norm_backward(one_grad, inputs, scale_one, norm_one)
    grad_tokens = middle_grad + input_part

    feeds = jnp.concatenate([sum_gate, sum_up, sum_down, sum_out], -1)
    owned = feeds[rank]
    for mask_z in range(1, ranks):
        owned = owned + swap(feeds[rank ^ mask_z].astype(BF16), "tensor", ranks, mask_z).astype(F32)
    owned_gate = owned[:, :units]
    owned_up = owned[:, wide : wide + units]
    owned_down = owned[:, 2 * wide : 2 * wide + units].T
    owned_out = owned[:, 3 * wide :].T

    low, high = mixer_sums
    first = lax.ppermute(
        jnp.where(rank < 2, high, low).astype(BF16), "tensor", [(0, 1), (1, 3), (3, 2), (2, 0)])
    second = lax.ppermute(jnp.where(rank == 2, high, low).astype(BF16), "tensor", [(2, 1), (1, 2)])
    third = jnp.where(rank == 0, low, jnp.where(rank == 3, high, second.astype(F32)))
    mixer_owned = first.astype(F32) + third

    def place(total, values, columns):
        for shard, value in zip(shard_ids, values):
            total = lax.dynamic_update_slice_in_dim(total, value, shard * columns, total.ndim - 1)
        return total

    pieces = [
        grad_norm_one, grad_norm_two, smalls_grads[0][4][0] + smalls_grads[1][4][0],
        place(jnp.zeros_like(filter_query), [g[0][:4] for g in smalls_grads], WIDE_K),
        place(jnp.zeros_like(filter_key), [g[1][:4] for g in smalls_grads], WIDE_K),
        place(jnp.zeros_like(filter_value), [g[2][:4] for g in smalls_grads], WIDE_V),
        place(jnp.zeros_like(decay_log), [g[3][0, :HEADS] for g in smalls_grads], HEADS),
        place(jnp.zeros_like(decay_bias), [g[3][1, :HEADS] for g in smalls_grads], HEADS),
    ]
    sizes = [p.size for p in pieces]
    length = -(-sum(sizes) // 1024) * 1024
    flat = jnp.concatenate([p.reshape(-1) for p in pieces] + [jnp.zeros((length - sum(sizes),), F32)])
    flat = flat.reshape(-1, LANES)
    bit = 1
    while bit < devices:
        flat = flat + swap(flat, "dp", devices, bit)
        bit *= 2
    bit = 1
    while bit < ranks:
        flat = flat + swap(flat, "tensor", ranks, bit)
        bit *= 2
    flat = flat.reshape(-1)
    summed, at = [], 0
    for piece, size in zip(pieces, sizes):
        summed.append(flat[at : at + size].reshape(piece.shape))
        at += size
    sum_one, sum_two, sum_gain, sum_fq, sum_fk, sum_fv, sum_log, sum_bias = summed
    edges = [WIDE_K, 2 * WIDE_K, 2 * WIDE_K + WIDE_V, WIDTH - LANES, WIDTH - LANES + HEADS]
    return (
        block_out, grad_tokens, sum_one,
        mixer_owned[:, : edges[0]],
        mixer_owned[:, edges[0] : edges[1]],
        mixer_owned[:, edges[1] : edges[2]],
        mixer_owned[:, edges[2] : edges[3]],
        mixer_owned[:, edges[3] : edges[4]],
        mixer_owned[:, edges[4] : edges[4] + HEADS],
        sum_fq, sum_fk, sum_fv, sum_log, sum_bias, sum_gain,
        owned_out, sum_two, owned_gate, owned_up, owned_down,
    )


def solution(mesh):
    placed = (
        P(("dp", "tensor"), None),
        P("dp"),
        P("dp"),
        P(),
        P("dp", "tensor"),
        P("dp", "tensor"),
        P("dp", "tensor"),
        P("dp", "tensor"),
        P("dp", "tensor"),
        P("dp", "tensor"),
        P(),
        P(),
        P(),
        P(),
        P(),
        P(),
        P("tensor", "dp"),
        P(),
        P("dp", "tensor"),
        P("dp", "tensor"),
        P("tensor", "dp"),
        P(("dp", "tensor"), None),
    )
    return jax.shard_map(
        shards,
        mesh=mesh,
        in_specs=placed,
        out_specs=(
            P(("dp", "tensor"), None),
            P(("dp", "tensor"), None),
            P(),
            P("dp", "tensor"),
            P("dp", "tensor"),
            P("dp", "tensor"),
            P("dp", "tensor"),
            P("dp", "tensor"),
            P("dp", "tensor"),
            P(),
            P(),
            P(),
            P(),
            P(),
            P(),
            P("tensor", "dp"),
            P(),
            P("dp", "tensor"),
            P("dp", "tensor"),
            P("tensor", "dp"),
        ),
        check_vma=False,
    )
```

```python
import functools
import jax
import jax.numpy as jnp
from jax import lax
from jax.experimental import pallas as pl
from jax.experimental.pallas import tpu as pltpu
from jax.sharding import PartitionSpec as P


DK = 128
DV = 256
SLOT = 1024
LANES = 128
BLOCK = 256
HEADS = 2
WIDE_K = HEADS * DK
WIDE_V = HEADS * DV
WIDTH = 2 * WIDE_K + 2 * WIDE_V + LANES
F32 = jnp.float32
BF16 = jnp.bfloat16


def dot(left, right, dim_left, dim_right):
    return lax.dot_general(
        left, right, (((dim_left,), (dim_right,)), ((), ())), preferred_element_type=F32
    )


def halves(value):
    high = value.astype(BF16)
    return high, (value - high.astype(F32)).astype(BF16)


def mm(left, right, dim_left=1, dim_right=0):
    left_high, left_low = halves(left)
    right_high, right_low = halves(right)
    return (
        dot(left_high, right_high, dim_left, dim_right)
        + dot(left_high, right_low, dim_left, dim_right)
        + dot(left_low, right_high, dim_left, dim_right)
    )


def mm_full(left, right, dim_left, dim_right):
    return lax.dot_general(
        left,
        right,
        (((dim_left,), (dim_right,)), ((), ())),
        preferred_element_type=F32,
        precision=lax.Precision.HIGHEST,
    )


def sigmoid(value):
    return 1.0 / (1.0 + jnp.exp(-value))


def softplus(value):
    return jnp.maximum(value, 0.0) + jnp.log1p(jnp.exp(-jnp.abs(value)))


def valid_rows(first, count, start, end):
    position = first + lax.broadcasted_iota(jnp.int32, (count, 1), 0)
    return jnp.where((position >= start) & (position < end), 1.0, 0.0).astype(F32)


def convolve(extended, taps, count):
    total = taps[0:1, :] * extended[5 : 5 + count]
    for offset in range(1, 4):
        total = total + taps[offset : offset + 1, :] * extended[5 + offset : 5 + offset + count]
    return total


def unit_scale(value):
    return lax.rsqrt(jnp.sum(value * value, -1, keepdims=True) + 1e-06)


def triangle(size):
    row = lax.broadcasted_iota(jnp.int32, (size, size), 0)
    column = lax.broadcasted_iota(jnp.int32, (size, size), 1)
    return row, column


def lower_ones(size):
    row, column = triangle(size)
    return jnp.where(row >= column, 1.0, 0.0).astype(F32)


def inverses(systems, size):
    row, column = triangle(size)
    differ = jnp.bitwise_xor(row, column)
    eye = jnp.where(differ == 0, 1.0, 0.0).astype(F32)
    found = [eye - jnp.where(differ == 1, system, 0.0) for system in systems]
    width = 2
    while width < size:
        mask = (differ >= width) & (differ < 2 * width)
        parts = [jnp.where(mask, system, 0.0) for system in systems]
        middle = [mm(f, p) for f, p in zip(found, parts)]
        found = [f - mm(m, f) for f, m in zip(found, middle)]
        width *= 2
    return found


def gather_inputs(first, start, end, refs, block):
    pre_q, pre_k, pre_v, pre_ab, halo_q, halo_k, halo_v, taps_q, taps_k, taps_v, rate, bias = refs
    valid = valid_rows(first, block, start, end)
    halo_valid = valid_rows(first - 8, 8, start, end)
    ext_q = jnp.concatenate([halo_q[...] * halo_valid, pre_q[...] * valid], 0)
    ext_k = jnp.concatenate([halo_k[...] * halo_valid, pre_k[...] * valid], 0)
    ext_v = jnp.concatenate([halo_v[...] * halo_valid, pre_v[...] * valid], 0)
    conv_q = convolve(ext_q, taps_q[...], block)
    conv_k = convolve(ext_k, taps_k[...], block)
    conv_v = convolve(ext_v, taps_v[...], block)
    both = pre_ab[...]
    shifted = both + bias[...]
    decay = rate[...] * softplus(shifted) * valid
    strength = sigmoid(both) * valid
    ones = lower_ones(block)
    cum = mm_full(ones, decay, 1, 0)
    cum_rows = mm_full(decay, ones, 0, 1)
    return dict(
        valid=valid, ext=(ext_q, ext_k, ext_v), conv=(conv_q, conv_k, conv_v), shifted=shifted,
        decay=decay, strength=strength, ones=ones, cum=cum, cum_rows=cum_rows,
    )


def head_operands(common, head, heads, block):
    conv_q, conv_k, conv_v = common["conv"]
    keys = slice(head * DK, (head + 1) * DK)
    vals = slice(head * DV, (head + 1) * DV)
    u_q, u_k, u_v = conv_q[:, keys], conv_k[:, keys], conv_v[:, vals]
    s_q, s_k, s_v = sigmoid(u_q), sigmoid(u_k), sigmoid(u_v)
    y_q, y_k = u_q * s_q, u_k * s_k
    n_q, n_k = unit_scale(y_q), unit_scale(y_k)
    cum = common["cum"][:, head : head + 1]
    cum_row = common["cum_rows"][head : head + 1, :]
    last = common["cum"][block - 1 : block, head : head + 1]
    spread = jnp.exp(jnp.minimum(cum - cum_row, 0.0))
    return dict(
        u=(u_q, u_k, u_v), s=(s_q, s_k, s_v), n=(n_q, n_k), unit=(y_q * n_q, y_k * n_k),
        q=y_q * (n_q * DK ** (-0.5)), k=y_k * (n_k * common["valid"]), v=u_v * s_v,
        beta=common["strength"][:, heads + head : heads + head + 1],
        growth=jnp.exp(cum), remain=jnp.exp(last - cum), whole=jnp.exp(last), spread=spread,
    )


def forward_kernel(heads, block, bounds, pre_q, pre_k, pre_v, pre_g, pre_ab, halo_q, halo_k, halo_v,
                   taps_q, taps_k, taps_v, rate, bias, gain, mixed, out, states, deltas, solves, state):
    row, step = pl.program_id(0), pl.program_id(1)

    @pl.when(step == 0)
    def _():
        state[...] = jnp.zeros_like(state)

    refs = (pre_q, pre_k, pre_v, pre_ab, halo_q, halo_k, halo_v, taps_q, taps_k, taps_v, rate, bias)
    common = gather_inputs(step * block, bounds[0, row], bounds[1, row], refs, block)
    ops = [head_operands(common, head, heads, block) for head in range(heads)]
    at, to = triangle(block)
    systems = [jnp.where(at > to, o["beta"] * o["spread"] * mm(o["k"], o["k"], 1, 1), 0.0) for o in ops]
    found = inverses(systems, block)
    for head, o in enumerate(ops):
        vals = slice(head * DV, (head + 1) * DV)
        old = state[head]
        states[head] = old.astype(states.dtype)
        source = o["beta"] * o["v"] - (o["beta"] * o["growth"]) * mm(o["k"], old)
        delta = mm(found[head], source)
        scores = jnp.where(at >= to, o["spread"] * mm(o["q"], o["k"], 1, 1), 0.0)
        emitted = o["growth"] * mm(o["q"], old) + mm(scores, delta)
        state[head] = o["whole"] * old + mm(o["k"] * o["remain"], delta, 0, 0)
        solves[head] = found[head].astype(solves.dtype)
        deltas[:, vals] = delta.astype(deltas.dtype)
        out[:, vals] = emitted.astype(out.dtype)
        scale = lax.rsqrt(jnp.mean(emitted * emitted, -1, keepdims=True) + 1e-05)
        gate = pre_g[:, vals]
        mixed[:, vals] = (
            emitted * scale * gain[...] * (gate * sigmoid(gate)) * common["valid"]
        ).astype(mixed.dtype)


def backward_kernel(heads, block, steps, bounds, pre_q, pre_k, pre_v, pre_g, pre_ab, halo_q, halo_k, halo_v,
                    taps_q, taps_k, taps_v, rate, bias, gain, out, states, deltas, solves, grad,
                    d_pre, d_taps_q, d_taps_k, d_taps_v, d_small, d_gain,
                    d_state, next_q, next_k, next_v):
    d_q = d_pre.at[:, 0:WIDE_K]
    d_k = d_pre.at[:, WIDE_K : 2 * WIDE_K]
    d_v = d_pre.at[:, 2 * WIDE_K : 2 * WIDE_K + WIDE_V]
    d_g = d_pre.at[:, 2 * WIDE_K + WIDE_V : 2 * WIDE_K + 2 * WIDE_V]
    d_ab = d_pre.at[:, 2 * WIDE_K + 2 * WIDE_V : WIDTH]
    row, back = pl.program_id(0), pl.program_id(1)
    step = steps - 1 - back

    @pl.when((row == 0) & (back == 0))
    def _():
        for ref in (d_taps_q, d_taps_k, d_taps_v, d_small, d_gain):
            ref[...] = jnp.zeros_like(ref)

    @pl.when(back == 0)
    def _():
        for ref in (d_state, next_q, next_k, next_v):
            ref[...] = jnp.zeros_like(ref)

    refs = (pre_q, pre_k, pre_v, pre_ab, halo_q, halo_k, halo_v, taps_q, taps_k, taps_v, rate, bias)
    common = gather_inputs(step * block, bounds[0, row], bounds[1, row], refs, block)
    valid = common["valid"]
    at, to = triangle(block)
    lane = lax.broadcasted_iota(jnp.int32, (block, LANES), 1)
    ones_cols = jnp.ones((block, LANES), BF16)
    d_cum = jnp.zeros((block, LANES), F32)
    d_last = jnp.zeros((1, LANES), F32)
    d_beta = jnp.zeros((block, LANES), F32)
    du_q, du_k, du_v = [], [], []
    gain_sum = jnp.zeros((1, DV), F32)
    for head in range(heads):
        o = head_operands(common, head, heads, block)
        vals = slice(head * DV, (head + 1) * DV)
        q, k, v, beta, growth, remain, whole, spread = (
            o[name] for name in ("q", "k", "v", "beta", "growth", "remain", "whole", "spread"))
        emitted = out[:, vals].astype(F32)
        scale = lax.rsqrt(jnp.mean(emitted * emitted, -1, keepdims=True) + 1e-05)
        unit = emitted * scale
        gate = pre_g[:, vals]
        s_g = sigmoid(gate)
        d_mixed = grad[:, vals].astype(F32) * valid
        d_g[:, vals] = (d_mixed * unit * gain[...] * (s_g * (1.0 + gate * (1.0 - s_g)))).astype(d_g.dtype)
        part = d_mixed * (gate * s_g)
        gain_sum = gain_sum + jnp.sum(part * unit, 0, keepdims=True)
        weighted = part * gain[...]
        d_out = scale * (weighted - unit * jnp.mean(weighted * unit, -1, keepdims=True))
        old = states[head].astype(F32)
        delta = deltas[:, vals]
        solve = solves[head]
        d_new = d_state[head]
        q_k = mm(q, k, 1, 1)
        k_k = mm(k, k, 1, 1)
        scores = jnp.where(at >= to, spread * q_k, 0.0)
        linked = jnp.where(at > to, spread * k_k, 0.0)
        k_s = mm(k, old)
        q_s = mm(q, old)
        k_rem = k * remain
        d_delta = mm(scores, d_out, 0, 0) + mm(k_rem, d_new)
        d_source = mm(solve, d_delta, 0, 0)
        d_system = -mm(d_source, delta, 1, 1)
        d_scores = mm(d_out, delta, 1, 1)
        d_qk = jnp.where(at >= to, d_scores * spread, 0.0)
        by_link = d_system * linked
        d_kk = jnp.where(at > to, beta * d_system * spread, 0.0)
        edge, edge_low = halves(d_scores * scores + beta * by_link)
        d_query = growth * mm(d_out, old, 1, 1) + mm(d_qk, k)
        back_state = mm(delta, d_new, 1, 1)
        d_key = (
            mm((beta * growth) * d_source, old, 1, 1) * (-1.0)
            + mm(d_qk, q, 0, 0)
            + mm(d_kk, k)
            + mm(d_kk, k, 0, 0)
            + remain * back_state
        )
        d_value = beta * d_source
        lose = jnp.sum(k_rem * back_state, -1, keepdims=True)
        pull = jnp.sum(d_source * k_s, -1, keepdims=True)
        grow = growth * (jnp.sum(d_out * q_s, -1, keepdims=True) - beta * pull)
        d_b = jnp.sum(d_source * v, -1, keepdims=True) - growth * pull + jnp.sum(by_link, -1, keepdims=True)
        cut = (
            dot(edge, ones_cols, 1, 0) - dot(edge, ones_cols, 0, 0)
            + dot(edge_low, ones_cols, 1, 0) - dot(edge_low, ones_cols, 0, 0)
        )
        d_cum = jnp.where(lane == head, cut + (grow - lose), d_cum)
        d_beta = jnp.where(lane == heads + head, d_b, d_beta)
        total = jnp.sum(lose, keepdims=True) + whole * jnp.sum(old * d_new, keepdims=True)
        d_last = jnp.where(lane[0:1] == head, total, d_last)
        d_state[head] = (
            whole * d_new + mm(q, growth * d_out, 0, 0) - mm(k * (beta * growth), d_source, 0, 0)
        )
        unit_q, unit_k = o["unit"]
        n_q, n_k = o["n"]
        d_unit = d_query * DK ** (-0.5)
        d_yq = n_q * (d_unit - unit_q * jnp.sum(unit_q * d_unit, -1, keepdims=True))
        d_unit = d_key * valid
        d_yk = n_k * (d_unit - unit_k * jnp.sum(unit_k * d_unit, -1, keepdims=True))
        for store, d_y, u, s in zip((du_q, du_k, du_v), (d_yq, d_yk, d_value), o["u"], o["s"]):
            store.append(d_y * (s * (1.0 + u * (1.0 - s))))
    d_decay = mm_full(common["ones"], d_cum, 0, 0) + d_last
    slope = d_decay * rate[...] * sigmoid(common["shifted"]) * valid
    strength = common["strength"]
    d_pre_b = d_beta * strength * (1.0 - strength)
    d_ab[...] = (slope + d_pre_b).astype(d_ab.dtype)
    d_small[0:1, :] += jnp.sum(d_decay * common["decay"], 0, keepdims=True)
    d_small[1:2, :] += jnp.sum(slope, 0, keepdims=True)
    d_gain[0:1, :] += gain_sum
    for store, ext, taps, d_taps, later, target in zip(
        (du_q, du_k, du_v), common["ext"], (taps_q, taps_k, taps_v), (d_taps_q, d_taps_k, d_taps_v),
        (next_q, next_k, next_v), (d_q, d_k, d_v),
    ):
        du = jnp.concatenate(store, 1) if heads > 1 else store[0]
        longer = jnp.concatenate([du, later[...]], 0)
        later[...] = du[0:8]
        total = taps[3:4, :] * du
        for offset in range(3):
            total = total + taps[offset : offset + 1, :] * longer[3 - offset : 3 - offset + block]
        target[...] = (total * valid).astype(target.dtype)
        for offset in range(4):
            d_taps[offset : offset + 1, :] += jnp.sum(du * ext[5 + offset : 5 + offset + block], 0, keepdims=True)


def pre_specs(place):
    def tile(width, column):
        return pl.BlockSpec((None, BLOCK, width), lambda r, c, *_: (r, place(c), column))

    def halo(width, column):
        return pl.BlockSpec(
            (None, 8, width),
            lambda r, c, *_: (r, jnp.maximum(place(c) * (BLOCK // 8) - 1, 0), column),
        )

    def fixed(rows, width):
        return pl.BlockSpec((rows, width), lambda r, c, *_: (0, 0))

    return [
        tile(WIDE_K, 0), tile(WIDE_K, 1), tile(WIDE_V, 1), tile(WIDE_V, 2),
        tile(LANES, (WIDTH - LANES) // LANES),
        halo(WIDE_K, 0), halo(WIDE_K, 1), halo(WIDE_V, 1),
        fixed(8, WIDE_K), fixed(8, WIDE_K), fixed(8, WIDE_V),
        fixed(1, LANES), fixed(1, LANES), fixed(1, DV),
    ]


def mixer_forward(bounds, pre, small):
    rows = pre.shape[0]
    steps = SLOT // BLOCK
    tile_v = pl.BlockSpec((None, BLOCK, WIDE_V), lambda r, c, *_: (r, c, 0))
    return pl.pallas_call(
        functools.partial(forward_kernel, HEADS, BLOCK),
        grid_spec=pltpu.PrefetchScalarGridSpec(
            num_scalar_prefetch=1,
            grid=(rows, steps),
            in_specs=pre_specs(lambda c: c),
            out_specs=[
                tile_v, tile_v,
                pl.BlockSpec((None, None, HEADS, DK, DV), lambda r, c, *_: (r, c, 0, 0, 0)),
                tile_v,
                pl.BlockSpec((None, None, HEADS, BLOCK, BLOCK), lambda r, c, *_: (r, c, 0, 0, 0)),
            ],
            scratch_shapes=[pltpu.VMEM((HEADS, DK, DV), F32)],
        ),
        out_shape=[
            jax.ShapeDtypeStruct((rows, SLOT, WIDE_V), BF16),
            jax.ShapeDtypeStruct((rows, SLOT, WIDE_V), F32),
            jax.ShapeDtypeStruct((rows, steps, HEADS, DK, DV), F32),
            jax.ShapeDtypeStruct((rows, SLOT, WIDE_V), F32),
            jax.ShapeDtypeStruct((rows, steps, HEADS, BLOCK, BLOCK), F32),
        ],
        cost_estimate=pl.CostEstimate(
            flops=10**10 * rows, bytes_accessed=2 * 10**7 * rows, transcendentals=10**7 * rows),
        name="mixer_forward",
    )(bounds, *[pre] * 8, *small)


def mixer_backward(bounds, pre, small, saved, grad):
    rows = pre.shape[0]
    steps = SLOT // BLOCK

    def tile(width):
        return pl.BlockSpec((None, BLOCK, width), lambda r, c, *_: (r, steps - 1 - c, 0))

    def fixed(rows, width):
        return pl.BlockSpec((rows, width), lambda r, c, *_: (0, 0))

    return pl.pallas_call(
        functools.partial(backward_kernel, HEADS, BLOCK, steps),
        grid_spec=pltpu.PrefetchScalarGridSpec(
            num_scalar_prefetch=1,
            grid=(rows, steps),
            in_specs=pre_specs(lambda c: steps - 1 - c) + [
                tile(WIDE_V),
                pl.BlockSpec((None, None, HEADS, DK, DV), lambda r, c, *_: (r, steps - 1 - c, 0, 0, 0)),
                tile(WIDE_V),
                pl.BlockSpec((None, None, HEADS, BLOCK, BLOCK), lambda r, c, *_: (r, steps - 1 - c, 0, 0, 0)),
                tile(WIDE_V),
            ],
            out_specs=[
                tile(WIDTH),
                fixed(8, WIDE_K), fixed(8, WIDE_K), fixed(8, WIDE_V), fixed(8, LANES), fixed(8, DV),
            ],
            scratch_shapes=[
                pltpu.VMEM((HEADS, DK, DV), F32),
                pltpu.VMEM((8, WIDE_K), F32), pltpu.VMEM((8, WIDE_K), F32), pltpu.VMEM((8, WIDE_V), F32),
            ],
        ),
        out_shape=[
            jax.ShapeDtypeStruct((rows, SLOT, WIDTH), BF16),
            jax.ShapeDtypeStruct((8, WIDE_K), F32),
            jax.ShapeDtypeStruct((8, WIDE_K), F32),
            jax.ShapeDtypeStruct((8, WIDE_V), F32),
            jax.ShapeDtypeStruct((8, LANES), F32),
            jax.ShapeDtypeStruct((8, DV), F32),
        ],
        cost_estimate=pl.CostEstimate(
            flops=10**10 * rows, bytes_accessed=2 * 10**7 * rows, transcendentals=10**7 * rows),
        name="mixer_backward",
    )(bounds, *[pre] * 8, *small, *saved, grad)


def matmul(left, right):
    return jnp.dot(left, right, preferred_element_type=F32)


def matmul_t(left, right):
    return lax.dot_general(left, right, (((1,), (1,)), ((), ())), preferred_element_type=F32)


def inner(left, right):
    return lax.dot_general(left, right, (((0,), (0,)), ((), ())), preferred_element_type=F32)


def norm_backward(grad_normed, inputs, scale, gain):
    unit = inputs * scale
    weighted = grad_normed * gain
    grad_gain = jnp.sum(grad_normed * unit, 0)
    grad_inputs = scale * (weighted - unit * jnp.mean(weighted * unit, -1, keepdims=True))
    return (grad_inputs, grad_gain)


def swap(value, axis, size, mask):
    return lax.ppermute(value, axis, [(i, i ^ mask) for i in range(size)])


def relative_order(devices):
    return list(range(0, devices, 2)) + list(range(1, devices, 2))


def relative_matrix(width, devices, me):
    block = width // devices
    order = jnp.array(relative_order(devices), jnp.int32)
    column = jnp.arange(width, dtype=jnp.int32)
    source = jnp.bitwise_xor(jnp.repeat(order, block), me) * block + column % block
    return (jnp.arange(width, dtype=jnp.int32)[:, None] == source[None, :]).astype(BF16)


def scatter_sum(left, right, devices):
    half = left.shape[1] // 2
    block = half * 2 // devices
    got = swap(inner(left[:, half:], right).astype(BF16), "dp", devices, 1)
    keep = inner(left[:, :half], right) + got.astype(F32)
    count, stride = devices // 2, 2
    while count > 1:
        ways = min(4, count)
        shaped = keep.reshape(count // ways, ways, block, keep.shape[-1])
        keep = shaped[:, 0]
        for way in range(1, ways):
            got = swap(shaped[:, way].astype(BF16), "dp", devices, way * stride)
            keep = keep + got.astype(F32)
        count //= ways
        stride *= ways
        keep = keep.reshape(count * block, keep.shape[-1])
    return keep


def gather_relative(value, devices):
    count, stride = devices // 2, 2
    while count > 1:
        ways = min(4, count)
        parts = [value]
        for way in range(1, ways):
            parts.append(swap(value, "dp", devices, way * stride))
        value = jnp.concatenate(parts, 0)
        count //= ways
        stride *= ways
    return value, swap(value, "dp", devices, 1)


def compute(
    tokens, lengths, starts, norm_one, w_query, w_key, w_value, w_gating, w_decay, w_strength,
    filter_query, filter_key, filter_value, decay_log, decay_bias, head_gain, w_output, norm_two,
    w_gate, w_up, w_down, cotangent,
):
    rank, me = lax.axis_index("tensor"), lax.axis_index("dp")
    ranks, devices = lax.axis_size("tensor"), lax.axis_size("dp")
    tok_dev, width = tokens.shape
    units = w_gate.shape[1]
    wide = -(-units // LANES) * LANES
    half = rank % 2
    row = rank // 2
    slot_pos = jnp.arange(SLOT, dtype=jnp.int32)
    row_mask = (
        (slot_pos[None, :] >= starts[:, None]) & (slot_pos[None, :] < (starts + lengths)[:, None])
    ).astype(F32)
    mask = lax.dynamic_slice_in_dim(row_mask.reshape(-1), rank * tok_dev, tok_dev)[:, None]
    bounds = lax.dynamic_slice_in_dim(jnp.stack([starts, starts + lengths]), row, 1, 1)

    def both_halves(mine, other):
        return jnp.where(half == 0, jnp.concatenate([mine, other], 0), jnp.concatenate([other, mine], 0))

    def exchange(value):
        return swap(value, "tensor", ranks, 1)

    inputs = tokens.astype(F32)
    scale_one = lax.rsqrt(jnp.mean(inputs * inputs, -1, keepdims=True) + 1e-05)
    normed_one = (inputs * scale_one * norm_one).astype(BF16)
    relative = relative_matrix(width, devices, me)

    def to_relative(value):
        return matmul(value, relative).astype(BF16)

    one_local = to_relative(normed_one)
    one_rel = both_halves(one_local, exchange(one_local))

    spare = jnp.zeros((w_query.shape[0], LANES - 2 * HEADS), BF16)
    packed = jnp.concatenate([w_query, w_key, w_value, w_gating, w_decay, w_strength, spare], 1)
    first = lax.ppermute(packed, "tensor", [(1, 0), (3, 1), (2, 3), (0, 2)])
    second = lax.ppermute(packed, "tensor", [(1, 2), (2, 1)])
    lower = jnp.where(rank == 0, packed, jnp.where(rank == 1, second, first))
    upper = jnp.where(rank == 3, packed, jnp.where(rank == 2, second, first))
    mixer_weights = [gather_relative(w, devices) for w in (lower, upper)]

    def gather(value):
        whole = lax.all_gather(value, ("tensor", "dp"), axis=0, tiled=True)
        return whole.reshape(ranks, width, value.shape[1])

    pad = ((0, 0), (0, wide - units))
    out_t = gather(w_output.T)
    gate_w = gather(jnp.pad(w_gate, pad))
    up_w = gather(jnp.pad(w_up, pad))
    down_t = gather(jnp.pad(w_down.T, pad))

    def small_of(shard):
        def taps(values, columns):
            return jnp.pad(lax.dynamic_slice_in_dim(values, shard * columns, columns, 1), ((0, 4), (0, 0)))

        log = lax.dynamic_slice_in_dim(decay_log, shard * HEADS, HEADS)
        bias = lax.dynamic_slice_in_dim(decay_bias, shard * HEADS, HEADS)
        return (
            taps(filter_query, WIDE_K), taps(filter_key, WIDE_K), taps(filter_value, WIDE_V),
            jnp.pad(-jnp.exp(log), (0, LANES - HEADS))[None],
            jnp.pad(bias, (0, LANES - HEADS))[None],
            head_gain[None],
        )

    shard_ids = [2 * half, 2 * half + 1]
    smalls = [small_of(s) for s in shard_ids]
    near, far = one_rel[:, : width // 2], one_rel[:, width // 2 :]
    pres = [(matmul(near, w[0]) + matmul(far, w[1]))[None] for w in mixer_weights]
    saves, own, got = [], [], []
    for pre, small in zip(pres, smalls):
        mixed, *saved = mixer_forward(bounds, pre, small)
        saves.append(saved)
        own.append(lax.dynamic_slice_in_dim(mixed[0], half * tok_dev, tok_dev))
        got.append(exchange(lax.dynamic_slice_in_dim(mixed[0], (1 - half) * tok_dev, tok_dev)))
    mixed = [jnp.where(half == 0, a, b) for a, b in zip(own + got, got + own)]
    attention = matmul_t(mixed[0], out_t[0])
    for part, weight in zip(mixed[1:], out_t[1:]):
        attention = attention + matmul_t(part, weight)
    middle = inputs + attention
    scale_two = lax.rsqrt(jnp.mean(middle * middle, -1, keepdims=True) + 1e-05)
    normed_two = (middle * scale_two * norm_two).astype(BF16)

    residual_grad = cotangent.astype(F32) * mask
    feed_grad = residual_grad.astype(BF16)
    feed_rel = to_relative(feed_grad)
    two_rel = to_relative(normed_two)
    feed = None
    two_grad = None
    hiddens, gate_grads, up_grads = [], [], []
    for t in range(ranks):
        gate_pre = matmul(normed_two, gate_w[t])
        up_pre = matmul(normed_two, up_w[t])
        s = jax.nn.sigmoid(gate_pre)
        hidden = (gate_pre * s * up_pre).astype(BF16)
        hidden_grad = matmul(feed_grad, down_t[t])
        gate_grad = (hidden_grad * up_pre * s * (1.0 + gate_pre * (1.0 - s))).astype(BF16)
        up_grad = (hidden_grad * gate_pre * s).astype(BF16)
        hiddens.append(hidden)
        gate_grads.append(gate_grad)
        up_grads.append(up_grad)
        part = matmul_t(hidden, down_t[t])
        feed = part if feed is None else feed + part
        part = matmul_t(gate_grad, gate_w[t]) + matmul_t(up_grad, up_w[t])
        two_grad = part if two_grad is None else two_grad + part
    block_out = (mask * (middle + feed)).astype(BF16)

    def wide_sum(left, values):
        return scatter_sum(left, jnp.concatenate(values, 1), devices)

    sum_gate = wide_sum(two_rel, gate_grads)
    sum_up = wide_sum(two_rel, up_grads)
    sum_down = wide_sum(feed_rel, hiddens)

    middle_part, grad_norm_two = norm_backward(two_grad, middle, scale_two, norm_two)
    middle_grad = residual_grad + middle_part
    attention_grad = middle_grad.astype(BF16)
    mixed_grads = []
    for j in range(2):
        sent = matmul(attention_grad, out_t[2 * (1 - half) + j]).astype(BF16)
        kept = matmul(attention_grad, out_t[2 * half + j]).astype(BF16)
        mixed_grads.append(both_halves(kept, exchange(sent))[None])
    sum_out = wide_sum(to_relative(attention_grad), mixed)

    one_part = None
    mixer_sums, smalls_grads = [], []
    for j in range(2):
        d_pre, *d_small = mixer_backward(bounds, pres[j], smalls[j], saves[j], mixed_grads[j])
        d_pre = d_pre[0]
        smalls_grads.append(d_small)
        mixer_sums.append(scatter_sum(one_rel, d_pre, devices))
        part = [matmul_t(d_pre, w) for w in mixer_weights[j]]
        one_part = part if one_part is None else [a + b for a, b in zip(one_part, part)]
    one_part = jnp.concatenate(one_part, 1)
    one_kept = lax.dynamic_slice_in_dim(one_part, half * tok_dev, tok_dev)
    one_sent = lax.dynamic_slice_in_dim(one_part, (1 - half) * tok_dev, tok_dev)
    one_grad = one_kept + exchange(one_sent.astype(BF16)).astype(F32)
    one_grad = sum(matmul_t(piece, relative) for piece in halves(one_grad))
    input_part, grad_norm_one = norm_backward(one_grad, inputs, scale_one, norm_one)
    grad_tokens = middle_grad + input_part

    def shard_part(value, t):
        size = value.shape[1] // ranks
        return value[:, t * size : (t + 1) * size]

    feeds = jnp.stack([
        jnp.concatenate([shard_part(v, t) for v in (sum_gate, sum_up, sum_down, sum_out)], 1)
        for t in range(ranks)
    ])
    owned = feeds[rank]
    for mask_z in range(1, ranks):
        owned = owned + swap(feeds[rank ^ mask_z].astype(BF16), "tensor", ranks, mask_z).astype(F32)
    owned_gate = owned[:, :units]
    owned_up = owned[:, wide : wide + units]
    owned_down = owned[:, 2 * wide : 2 * wide + units].T
    owned_out = owned[:, 3 * wide :].T

    low, high = mixer_sums
    first = lax.ppermute(
        jnp.where(rank < 2, high, low).astype(BF16), "tensor", [(0, 1), (1, 3), (3, 2), (2, 0)])
    second = lax.ppermute(jnp.where(rank == 2, high, low).astype(BF16), "tensor", [(2, 1), (1, 2)])
    third = jnp.where(rank == 0, low, jnp.where(rank == 3, high, second.astype(F32)))
    mixer_owned = first.astype(F32) + third

    def place(total, values, columns):
        for shard, value in zip(shard_ids, values):
            total = lax.dynamic_update_slice_in_dim(total, value, shard * columns, total.ndim - 1)
        return total

    pieces = [
        grad_norm_one, grad_norm_two, smalls_grads[0][4][0] + smalls_grads[1][4][0],
        place(jnp.zeros_like(filter_query), [g[0][:4] for g in smalls_grads], WIDE_K),
        place(jnp.zeros_like(filter_key), [g[1][:4] for g in smalls_grads], WIDE_K),
        place(jnp.zeros_like(filter_value), [g[2][:4] for g in smalls_grads], WIDE_V),
        place(jnp.zeros_like(decay_log), [g[3][0, :HEADS] for g in smalls_grads], HEADS),
        place(jnp.zeros_like(decay_bias), [g[3][1, :HEADS] for g in smalls_grads], HEADS),
    ]
    sizes = [p.size for p in pieces]
    length = -(-sum(sizes) // 1024) * 1024
    flat = jnp.concatenate([p.reshape(-1) for p in pieces] + [jnp.zeros((length - sum(sizes),), F32)])
    flat = flat.reshape(-1, LANES)
    bit = 1
    while bit < devices:
        flat = flat + swap(flat, "dp", devices, bit)
        bit *= 2
    bit = 1
    while bit < ranks:
        flat = flat + swap(flat, "tensor", ranks, bit)
        bit *= 2
    flat = flat.reshape(-1)
    summed, at = [], 0
    for piece, size in zip(pieces, sizes):
        summed.append(flat[at : at + size].reshape(piece.shape))
        at += size
    sum_one, sum_two, sum_gain, sum_fq, sum_fk, sum_fv, sum_log, sum_bias = summed
    edges = [WIDE_K, 2 * WIDE_K, 2 * WIDE_K + WIDE_V, WIDTH - LANES, WIDTH - LANES + HEADS]
    return (
        block_out, grad_tokens, sum_one,
        mixer_owned[:, : edges[0]],
        mixer_owned[:, edges[0] : edges[1]],
        mixer_owned[:, edges[1] : edges[2]],
        mixer_owned[:, edges[2] : edges[3]],
        mixer_owned[:, edges[3] : edges[4]],
        mixer_owned[:, edges[4] : edges[4] + HEADS],
        sum_fq, sum_fk, sum_fv, sum_log, sum_bias, sum_gain,
        owned_out, sum_two, owned_gate, owned_up, owned_down,
    )


def solution(mesh):
    placed = (
        P(("dp", "tensor"), None),
        P("dp"),
        P("dp"),
        P(),
        P("dp", "tensor"),
        P("dp", "tensor"),
        P("dp", "tensor"),
        P("dp", "tensor"),
        P("dp", "tensor"),
        P("dp", "tensor"),
        P(),
        P(),
        P(),
        P(),
        P(),
        P(),
        P("tensor", "dp"),
        P(),
        P("dp", "tensor"),
        P("dp", "tensor"),
        P("tensor", "dp"),
        P(("dp", "tensor"), None),
    )
    return jax.shard_map(
        compute,
        mesh=mesh,
        in_specs=placed,
        out_specs=(
            P(("dp", "tensor"), None),
            P(("dp", "tensor"), None),
            P(),
            P("dp", "tensor"),
            P("dp", "tensor"),
            P("dp", "tensor"),
            P("dp", "tensor"),
            P("dp", "tensor"),
            P("dp", "tensor"),
            P(),
            P(),
            P(),
            P(),
            P(),
            P(),
            P("tensor", "dp"),
            P(),
            P("dp", "tensor"),
            P("dp", "tensor"),
            P("tensor", "dp"),
        ),
        check_vma=False,
    )
```
